32 devices in a mesh: alpha: 8 (over y, x, core), beta: 4 (over z).
Axes of the slice: x: 2, y: 2, z: 4, core: 2. Of those that a mesh axis runs over, the one named last changes fastest.
Arguments:
- coefficients: bfloat16 [4096, 4096], P('alpha', 'beta'), may hold values from -6 to 6
- couplings: bfloat16 [8, 256, 256], replicated, may hold values from -0.375 to 0.375
- exc_list: int32 [8, 8, 3], replicated, may hold values from 0 to 15, as said below
- counts: int32 [8, 8], replicated, may hold values from 0 to 1, as said below
- beta_tiles: bfloat16 [4, 1024, 4096], P(None, None, 'beta'), may hold values from -0.09375 to 0.09375
Outputs:
- sigma_vector: float32 [4096, 4096], P('alpha', 'beta')
The draws below stay inside these ranges and needn't reach their ends.
Inputs may be any that keep to these rules, and one draw needn't show every extreme that they name: `exc_list`: entry [s, p] describes the slot from alpha device s to alpha device p: field 0 is a source block held by device s (from s * 2 to s * 2 + 1), field 1 a target block held by device p (from p * 2 to p * 2 + 1), field 2 a coupling index below 8. `counts`: 1 where a slot is live, 0 where it is empty; in every draw some device p has a live slot from every device s.
All inputs are finite; a program needn't handle non-finite values.
Results may differ from the reference program's by a relative error of at most 0.0029.
Values may be sent and summed in bfloat16 or wider, within the bound.
A program may use at most 192 MiB of HBM per device.

```python
import jax
import jax.numpy as jnp
from jax import lax

AB = 256
BB = 1024
ABLK = 2
KC = 8
STOPS = 4
NA = 4096
NBETA = 4096
N_ALPHA = 8
N_BETA = 4


def route_tables(key):
    key = jax.random.fold_in(key, 7)
    key_dest, key_live, key_source, key_target, key_kind = jax.random.split(key, 5)
    full_dest = jax.random.randint(key_dest, (), 0, N_ALPHA)
    device_range = jnp.arange(N_ALPHA, dtype=jnp.int32)
    is_live = jax.random.randint(key_live, (N_ALPHA, N_ALPHA), 0, 5) < 2
    is_live = is_live | (device_range[None, :] == full_dest)
    occupancy = is_live.astype(jnp.int32)
    source = device_range[:, None] * ABLK + jax.random.randint(key_source, (N_ALPHA, N_ALPHA), 0, ABLK)
    target = device_range[None, :] * ABLK + jax.random.randint(key_target, (N_ALPHA, N_ALPHA), 0, ABLK)
    coupling_index = jax.random.randint(key_kind, (N_ALPHA, N_ALPHA), 0, KC)
    entries = jnp.stack([source, target, coupling_index], axis=-1).astype(jnp.int32)
    return (entries, occupancy)


def draw_exc_list(key, part):
    return route_tables(key)[0]


def draw_counts(key, part):
    return route_tables(key)[1]


def steps_of(key, extent, pieces, low, largest):
    def one(dim, blocks):
        draws = jax.random.uniform(jax.random.fold_in(jax.random.fold_in(key, 6), dim), (blocks,), jnp.float32, low / len(pieces), largest / len(pieces))
        return jnp.repeat(jnp.exp(draws), extent[dim] // blocks).reshape((-1,) + (1,) * (len(extent) - dim - 1))

    level = one(*pieces[0])
    for cut in pieces[1:]:
        level = level * one(*cut)
    return level


def noise(rng, shape, deviation, bound, cuts=(), kind=jnp.bfloat16):
    result = jax.random.normal(rng, shape, jnp.float32) * deviation
    if len(cuts) > 0:
        result = steps_of(rng, shape, cuts, -0.22, 0.18) * result
    return jnp.clip(result, min=-bound, max=bound).astype(kind)


def setup_inputs(seed: int = 0) -> dict:
    key_of = jax.random.split(jax.random.key(seed), 6)
    coefficients = noise(key_of[0], (NA, NBETA), 1.0, 6.0, ((0, 8), (1, 4)))
    couplings = noise(key_of[1], (KC, AB, AB), AB ** -0.5, 0.375)
    exc_list = draw_exc_list(jax.random.fold_in(key_of[5], 71), 0)
    counts = draw_counts(jax.random.fold_in(key_of[5], 71), 0)
    beta_tiles = noise(key_of[4], (STOPS, BB, NBETA), (STOPS * BB) ** -0.5, 0.09375, ((2, 4),))
    return dict(coefficients=coefficients, couplings=couplings, exc_list=exc_list, counts=counts, beta_tiles=beta_tiles)


def reference(coefficients, couplings, exc_list, counts, beta_tiles):
    block_count = ABLK * N_ALPHA
    blocks = coefficients.astype(jnp.float32).reshape(block_count, AB * NBETA)
    weights_cat = jnp.transpose(couplings.astype(jnp.float32), (1, 0, 2)).reshape(AB, KC * AB)
    coupling_range = jnp.arange(KC, dtype=jnp.int32)
    block_range = jnp.arange(block_count, dtype=jnp.int32)

    def one_target(target):
        owner_device = target // ABLK
        is_live = (counts[:, owner_device] == 1) & (exc_list[:, owner_device, 1] == target)
        source = exc_list[:, owner_device, 0]
        coupling_index = exc_list[:, owner_device, 2]
        onehot = ((coupling_index[None, :] == coupling_range[:, None]) & is_live[None, :]).astype(jnp.float32)
        source_hot = (source[:, None] == block_range[None, :]).astype(jnp.float32)
        grouping = jnp.dot(onehot, source_hot, precision=lax.Precision.HIGHEST)
        grouped = jnp.dot(grouping, blocks, precision=lax.Precision.HIGHEST).reshape(KC * AB, NBETA)
        return jnp.dot(weights_cat, grouped, precision=lax.Precision.HIGHEST).astype(jnp.bfloat16)

    interm = lax.map(one_target, jnp.arange(block_count, dtype=jnp.int32)).reshape(block_count * AB, NBETA)

    def one_column(column):
        summed = jnp.zeros((block_count * AB, BB), jnp.float32)
        for offset in range(STOPS):
            anchor = (column - offset) % N_BETA
            shifted = lax.dynamic_slice_in_dim(interm, (anchor * BB).astype(jnp.int32), BB, 1).astype(jnp.float32)
            tile_block = lax.dynamic_slice_in_dim(beta_tiles[offset], (column * BB).astype(jnp.int32), BB, 1).astype(jnp.float32)
            summed = summed + jnp.dot(shifted, tile_block, precision=lax.Precision.HIGHEST)
        return summed

    results = lax.map(one_column, jnp.arange(N_BETA, dtype=jnp.int32))
    return jnp.transpose(results, (1, 0, 2)).reshape(block_count * AB, N_BETA * BB)
```

```python
import functools

import jax
import jax.numpy as jnp
from jax import lax
from jax.experimental import pallas as pl
from jax.experimental.pallas import tpu as pltpu
from jax.sharding import PartitionSpec as P

MESH = pl.DeviceIdType.MESH
WIDTHS = (1, 2, 2, 2, 1)
TILE = 256
AHEAD = 1
SHARES = (4, 4, 4, 2, 2)
PIECES = 4
LANES = 128


def split(columns):
    unit = columns // sum(WIDTHS)
    widths = [unit * part for part in WIDTHS]
    return widths, [sum(widths[:c]) for c in range(len(widths))]


def flip(position, mask):
    bit = lax.rem(lax.div(position, mask), 2)
    return position + mask * (1 - 2 * bit)


def kernel(
    n_alpha, n_beta, rounds, chunks,
    exc_ref, counts_ref, coupling_ref, c_hbm, b_hbm, out_ref,
    weights, gathered, tiles, held, moved,
    send_sem, recv_sem, own_sem, zsend_sem, zrecv_sem, tile_sem,
):
    n_chips = n_alpha // 2
    n_blocks, order = c_hbm.shape[0], c_hbm.shape[1]
    n_stops = b_hbm.shape[0]
    widths, starts = split(out_ref.shape[1])
    alpha, beta = lax.axis_index("alpha"), lax.axis_index("beta")
    chip, core = lax.div(alpha, 2), lax.rem(alpha, 2)

    def mask_of(step, which):
        return (1 - which) * 2**step + which * 2 ** (rounds - 1 - step)

    def origin(label, which):
        source = chip
        for step in range(rounds):
            if (label >> step) & 1:
                source = flip(source, mask_of(step, which))
        return source * 2 + which

    if n_beta == n_stops:
        way, far, near = 1 - 2 * core, n_beta // 2, n_beta - 1 - n_beta // 2
    else:
        way, far, near = 1, n_stops - 1, 0
    ahead = lax.rem(beta + way + n_beta, n_beta)
    behind = lax.rem(beta - way + n_beta, n_beta)

    sibling = (alpha + 1 - 2 * core, beta)
    neighbours = [(flip(chip, mask_of(step, core)) * 2 + core, beta) for step in range(rounds)]
    greeted = neighbours + [sibling, (alpha, ahead), (alpha, behind)]
    barrier = pltpu.get_barrier_semaphore()
    for device in greeted:
        pl.semaphore_signal(barrier, inc=1, device_id=device, device_id_type=MESH)
    own = []
    for c in range(chunks):
        own.append(
            pltpu.make_async_copy(c_hbm.at[:, :, pl.ds(starts[c], widths[c])], held[c].at[0], own_sem.at[c])
        )
    own[0].start()
    pl.semaphore_wait(barrier, len(greeted))

    def to_alpha(c, label, target, device):
        source = c_hbm.at[:, :, pl.ds(starts[c], widths[c])] if label == 0 else held[c].at[label]
        return pltpu.make_async_remote_copy(
            src_ref=source,
            dst_ref=held[c].at[target],
            send_sem=send_sem.at[c, target],
            recv_sem=recv_sem.at[c, target],
            device_id=device,
            device_id_type=MESH,
        )

    copies = [{} for _ in range(chunks)]

    def pass_on(c, label):
        for step in range(label.bit_length(), rounds):
            target = label + 2**step
            copies[c][target] = to_alpha(c, label, target, neighbours[step])
            copies[c][target].start()
        target = n_chips + label
        copies[c][target] = to_alpha(c, label, target, sibling)
        copies[c][target].start()

    def slot_of(hop):
        return lax.rem(hop * way + n_beta * n_stops, n_beta)

    hops = [{} for _ in range(chunks)]

    def to_beta(c, kind, hop):
        sign, device, index = (1, ahead, hop - 1) if kind == "far" else (-1, behind, far + hop - 1)
        copy = pltpu.make_async_remote_copy(
            src_ref=moved[c].at[slot_of(sign * (hop - 1))],
            dst_ref=moved[c].at[slot_of(sign * hop)],
            send_sem=zsend_sem.at[c, index],
            recv_sem=zrecv_sem.at[c, index],
            device_id=(alpha, device),
            device_id_type=MESH,
        )
        hops[c][kind, hop] = copy
        copy.start()

    for c in range(min(AHEAD, chunks)):
        if c > 0:
            own[c].start()
        pass_on(c, 0)
    tile_copy = pltpu.make_async_copy(b_hbm, tiles, tile_sem)
    tile_copy.start()

    sources = [origin(label, core) for label in range(n_chips)]
    sources += [origin(label, 1 - core) for label in range(n_chips)]
    picked = []
    for slot, source in enumerate(sources):
        live = counts_ref[source, alpha] == 1
        picked.append(jnp.clip(exc_ref[0, source, alpha] - source * n_blocks, 0, n_blocks - 1))
        target = exc_ref[1, source, alpha] - alpha * n_blocks
        matrix = coupling_ref[exc_ref[2, source, alpha]]
        for block in range(n_blocks):
            keep = jnp.where(live & (target == block), 1.0, 0.0).astype(jnp.float32)
            weights[pl.ds(block * order, order), pl.ds(slot * order, order)] = (
                matrix.astype(jnp.float32) * keep
            ).astype(jnp.bfloat16)

    def product(c):
        @pl.loop(0, out_ref.shape[1] // TILE)
        def _(n):
            columns = pl.ds(pl.multiple_of(n * TILE, TILE), TILE)
            left = jnp.concatenate([moved[c][d] for d in range(n_stops)], axis=1)
            right = jnp.concatenate(
                [tiles[d, pl.ds(starts[c], widths[c]), columns] for d in range(n_stops)], axis=0
            )
            value = jnp.dot(left, right, preferred_element_type=jnp.float32)
            if c == 0:
                out_ref[:, columns] = value
            else:
                out_ref[:, columns] += value

    def relay(c):
        for kind, last in (("far", far), ("near", near)):
            for hop in range(1, last):
                hops[c][kind, hop].wait_recv()
                to_beta(c, kind, hop + 1)

    def finish(c):
        for kind, last in (("far", far), ("near", near)):
            if last > 0:
                hops[c][kind, last].wait_recv()
        if c == 0:
            tile_copy.wait()
        product(c)

    for c in range(chunks):
        for label in range(1, n_chips):
            copies[c][label].wait_recv()
            pass_on(c, label)
            if label == 1 and c + AHEAD < chunks:
                own[c + AHEAD].start()
                pass_on(c + AHEAD, 0)
        own[c].wait()
        for label in range(n_chips):
            copies[c][n_chips + label].wait_recv()
        for slot in range(n_alpha):
            gathered[pl.ds(slot * order, order), pl.ds(0, widths[c])] = held[c][slot, picked[slot]]
        moved[c][0] = jnp.dot(
            weights[...], gathered[:, pl.ds(0, widths[c])], preferred_element_type=jnp.float32
        ).astype(jnp.bfloat16)
        to_beta(c, "far", 1)
        if near > 0:
            to_beta(c, "near", 1)
        if c >= 1:
            relay(c - 1)
        if c >= 2:
            finish(c - 2)
    relay(chunks - 1)
    for c in range(max(chunks - 2, 0), chunks):
        finish(c)
    for c in range(chunks):
        for copy in copies[c].values():
            copy.wait_send()
        for copy in hops[c].values():
            copy.wait_send()


def line_kernel(
    n_alpha, n_beta, rounds, heights, early,
    exc_hbm, counts_hbm, coupling_hbm, c_hbm, b_hbm, out_ref,
    exc_ref, counts_ref, coupling_ref, weights, tiles, blocks, outer_tiles, partial, remote_sum, held, gathered,
    in_sem, raw_send, raw_recv, sum_send, sum_recv, tile_send, tile_recv, spread_send, spread_recv, send_sem, recv_sem,
):
    n_chips = n_alpha // 2
    n_blocks, order, columns = c_hbm.shape
    chunks = len(heights)
    offsets = [sum(heights[:c]) for c in range(chunks)]
    alpha, beta = lax.axis_index("alpha"), lax.axis_index("beta")
    chip, core = lax.div(alpha, 2), lax.rem(alpha, 2)
    side = lax.div(beta, 2)
    outer, inner = 3 * side, 1 + side
    across, beyond = 2 - side, 3 - 3 * side
    is_outer = beta == outer

    def mask_of(step, which):
        return (1 - which) * 2**step + which * 2 ** (rounds - 1 - step)

    def origin(label, which):
        source = chip
        for step in range(rounds):
            if (label >> step) & 1:
                source = flip(source, mask_of(step, which))
        return source * 2 + which

    def distance(source):
        return lax.rem(beta - source + n_beta, n_beta)

    sources = [origin(label, core) for label in range(n_chips)]
    sources += [origin(label, 1 - core) for label in range(n_chips)]
    sibling = (alpha + 1 - 2 * core, beta)
    neighbours = [(flip(chip, mask_of(step, core)) * 2 + core, beta) for step in range(rounds)]
    near = (alpha, is_outer.astype(jnp.int32) * inner + (1 - is_outer.astype(jnp.int32)) * outer)
    facing = (alpha, across)

    barrier = pltpu.get_barrier_semaphore()
    for device in neighbours + [sibling, near]:
        pl.semaphore_signal(barrier, inc=1, device_id=device, device_id_type=MESH)

    @pl.when(jnp.logical_not(is_outer))
    def _():
        pl.semaphore_signal(barrier, inc=1, device_id=facing, device_id_type=MESH)

    local = [
        pltpu.make_async_copy(exc_hbm, exc_ref, in_sem.at[0]),
        pltpu.make_async_copy(counts_hbm, counts_ref, in_sem.at[1]),
        pltpu.make_async_copy(coupling_hbm, coupling_ref, in_sem.at[2]),
        pltpu.make_async_copy(c_hbm, blocks.at[beta], in_sem.at[3]),
        pltpu.make_async_copy(b_hbm, tiles, in_sem.at[4]),
    ]
    for copy in local:
        copy.start()
    pl.semaphore_wait(barrier, rounds + 3 - is_outer.astype(jnp.int32))

    def rows_of(c):
        return pl.ds(offsets[c], heights[c])

    def remote(source, target, send, recv, device):
        return pltpu.make_async_remote_copy(
            src_ref=source, dst_ref=target, send_sem=send, recv_sem=recv, device_id=device, device_id_type=MESH
        )

    def raw(c, plane, kind, device):
        source = c_hbm.at[:, rows_of(c)] if kind < 2 else blocks.at[plane, :, rows_of(c)]
        return remote(
            source, blocks.at[plane, :, rows_of(c)], raw_send.at[kind, c], raw_recv.at[plane, c], device
        )

    def sum_copy(c):
        here = remote_sum.at[:, rows_of(c)]
        return remote(here, here, sum_send.at[c], sum_recv.at[c], near)

    piece = 2 * b_hbm.shape[1] // n_alpha
    part = piece // PIECES

    def tile_copy(q):
        row = alpha * piece + q * part
        which = lax.div(row, b_hbm.shape[1])
        tile = (1 - which) * 2 + which * (1 + 2 * side)
        source = b_hbm.at[tile, pl.ds(pl.multiple_of(lax.rem(row, b_hbm.shape[1]), part), part)]
        target = outer_tiles.at[pl.ds(pl.multiple_of(row, part), part)]
        return remote(source, target, tile_send.at[q], tile_recv.at[q], near)

    def tile_spread(q, label, target, device):
        here = outer_tiles.at[pl.ds(pl.multiple_of(sources[label] * piece + q * part, part), part)]
        return remote(here, here, spread_send.at[q, target], spread_recv.at[q, target], device)

    def held_spread(c, label, target, device):
        return remote(held[c].at[label], held[c].at[target], send_sem.at[c, target], recv_sem.at[c, target], device)

    def spread(make, index, label, sent):
        for step in range(label.bit_length(), rounds):
            sent.append(make(index, label, label + 2**step, neighbours[step]))
            sent[-1].start()
        sent.append(make(index, label, n_chips + label, sibling))
        sent[-1].start()

    def arrive(make, index, label):
        make(index, label, label, sibling).wait_recv()

    def tile_arrive(q, label):
        here = outer_tiles.at[pl.ds(pl.multiple_of(sources[label] * piece + q * part, part), part)]
        remote(here, here, spread_send.at[q, label], spread_recv.at[q, label], sibling).wait_recv()

    def set_weights():
        for copy in local[:3]:
            copy.wait()
        picked = []
        for slot, source in enumerate(sources):
            live = counts_ref[source, alpha] == 1
            picked.append(jnp.clip(exc_ref[0, source, alpha] - source * n_blocks, 0, n_blocks - 1))
            target = exc_ref[1, source, alpha] - alpha * n_blocks
            matrix = coupling_ref[exc_ref[2, source, alpha]]
            for block in range(n_blocks):
                keep = jnp.where(live & (target == block), 1.0, 0.0).astype(jnp.float32)
                value = (matrix.astype(jnp.float32) * keep).astype(jnp.bfloat16)
                for half in range(order // LANES):
                    weights[half, pl.ds(block * order, order), pl.ds(slot * LANES, LANES)] = value[
                        :, half * LANES : (half + 1) * LANES
                    ]
        return picked

    def product(c, terms, store):
        @pl.loop(0, columns // TILE)
        def _(n):
            at = pl.ds(pl.multiple_of(n * TILE, TILE), TILE)
            value = None
            for plane, right in terms:
                left = blocks[plane, :, rows_of(c)].reshape(n_blocks * heights[c], columns)
                term = jnp.dot(left, right(at), preferred_element_type=jnp.float32)
                value = term if value is None else value + term
            store(at, value)

    def own_tile(plane):
        return lambda at: tiles[distance(plane), :, at]

    def far_tile(k):
        return lambda at: outer_tiles[pl.ds(k * columns, columns), at]

    def store_held(c):
        def store(at, value):
            held[c][0, :, :, at] = value.astype(jnp.bfloat16).reshape(n_blocks, heights[c], TILE)
        return store

    def store_sum(c):
        def store(at, value):
            remote_sum[:, rows_of(c), at] = value.astype(jnp.bfloat16).reshape(n_blocks, heights[c], TILE)
        return store

    def store_partial(c):
        def store(at, value):
            partial[:, rows_of(c), at] = value.reshape(n_blocks, heights[c], TILE)
        return store

    def relay(c, label):
        arrive(held_spread, c, label)
        spread(held_spread, c, label, sent)

    def finish(c, picked):
        for label in range(n_chips):
            arrive(held_spread, c, n_chips + label)
        half, within = offsets[c] // LANES, offsets[c] % LANES
        for slot in range(n_alpha):
            gathered[half, pl.ds(slot * LANES + within, heights[c])] = held[c][slot, picked[slot]]
        if within + heights[c] == LANES:
            @pl.loop(0, columns // TILE)
            def _(n):
                at = pl.ds(pl.multiple_of(n * TILE, TILE), TILE)
                value = jnp.dot(weights[half], gathered[half, :, at], preferred_element_type=jnp.float32)
                if half == 0:
                    out_ref[:, at] = value
                else:
                    out_ref[:, at] += value

    def follow(c, picked):
        if c >= 1:
            for label in range(1, n_chips):
                relay(c - 1, label)
        if c >= 2:
            finish(c - 2, picked)

    def end(picked):
        for label in range(1, n_chips):
            relay(chunks - 1, label)
        for c in range(max(chunks - 2, 0), chunks):
            finish(c, picked)
        for copy in sent:
            copy.wait_send()

    sent = []

    def start(copy):
        sent.append(copy)
        copy.start()

    @pl.when(is_outer)
    def _():
        for q in range(PIECES):
            start(tile_copy(q))
        for c in range(chunks):
            start(raw(c, outer, 0, near))
        picked = set_weights()
        local[3].wait()
        local[4].wait()
        for c in range(chunks):
            raw(c, inner, 0, near).wait_recv()
            product(c, [(outer, own_tile(outer)), (inner, own_tile(inner))], store_partial(c))
        for c in range(chunks):
            sum_copy(c).wait_recv()
            held[c][0] = (
                partial[:, rows_of(c)] + remote_sum[:, rows_of(c)].astype(jnp.float32)
            ).astype(jnp.bfloat16)
            spread(held_spread, c, 0, sent)
            follow(c, picked)
        end(picked)

    sent = []

    @pl.when(jnp.logical_not(is_outer))
    def _():
        for c in range(chunks):
            start(raw(c, inner, 0, near))
        for c in range(early):
            start(raw(c, inner, 1, facing))
        picked = set_weights()
        for q in range(PIECES):
            tile_copy(q).wait_recv()
            spread(tile_spread, q, 0, sent)
            if q >= 1:
                for label in range(1, n_chips):
                    tile_arrive(q - 1, label)
                    spread(tile_spread, q - 1, label, sent)
        local[3].wait()
        local[4].wait()

        def pass_on(c):
            raw(c, outer, 0, near).wait_recv()
            start(raw(c, outer, 2, facing))
            if c + early < chunks:
                start(raw(c + early, inner, 1, facing))

        pass_on(0)
        for label in range(1, n_chips):
            tile_arrive(PIECES - 1, label)
            spread(tile_spread, PIECES - 1, label, sent)
        pass_on(1)
        for q in range(PIECES):
            for label in range(n_chips):
                tile_arrive(q, n_chips + label)
        for c in range(chunks):
            if c + 2 < chunks:
                pass_on(c + 2)
            raw(c, across, 1, facing).wait_recv()
            raw(c, beyond, 2, facing).wait_recv()
            product(c, [(across, far_tile(0)), (beyond, far_tile(1))], store_sum(c))
            start(sum_copy(c))
            product(c, [(plane, own_tile(plane)) for plane in (inner, outer, across, beyond)], store_held(c))
            spread(held_spread, c, 0, sent)
            follow(c, picked)
        end(picked)


def line_call(mesh, coefficients, couplings, exc_list, counts, beta_tiles):
    n_alpha, n_beta = mesh.shape["alpha"], mesh.shape["beta"]
    order = couplings.shape[1]
    rows, columns = coefficients.shape
    n_blocks = rows // order
    heights = [order * share // sum(SHARES) for share in SHARES]
    chunks = len(heights)
    hbm = pl.BlockSpec(memory_space=pl.ANY)
    dma = pltpu.SemaphoreType.DMA
    return pl.pallas_call(
        functools.partial(line_kernel, n_alpha, n_beta, (n_alpha // 2).bit_length() - 1, heights, 3),
        out_shape=pltpu.VMEM((rows, columns), jnp.float32),
        in_specs=[hbm] * 5,
        out_specs=pl.BlockSpec(memory_space=pltpu.VMEM),
        scratch_shapes=[
            pltpu.SMEM((3, n_alpha, n_alpha), jnp.int32),
            pltpu.SMEM((n_alpha, n_alpha), jnp.int32),
            pltpu.VMEM(couplings.shape, jnp.bfloat16),
            pltpu.VMEM((order // LANES, rows, n_alpha * LANES), jnp.bfloat16),
            pltpu.VMEM(beta_tiles.shape, jnp.bfloat16),
            pltpu.VMEM((n_beta, n_blocks, order, columns), jnp.bfloat16),
            pltpu.VMEM((2 * columns, columns), jnp.bfloat16),
            pltpu.VMEM((n_blocks, order, columns), jnp.float32),
            pltpu.VMEM((n_blocks, order, columns), jnp.bfloat16),
            [pltpu.VMEM((n_alpha, n_blocks, height, columns), jnp.bfloat16) for height in heights],
            pltpu.VMEM((order // LANES, n_alpha * LANES, columns), jnp.bfloat16),
            dma((5,)),
            dma((3, chunks)),
            dma((n_beta, chunks)),
            dma((chunks,)),
            dma((chunks,)),
            dma((PIECES,)),
            dma((PIECES,)),
            dma((PIECES, n_alpha)),
            dma((PIECES, n_alpha)),
            dma((chunks, n_alpha)),
            dma((chunks, n_alpha)),
        ],
        compiler_params=pltpu.CompilerParams(
            collective_id=0, has_side_effects=True, vmem_limit_bytes=60 * 2**20
        ),
    )(
        exc_list.transpose(2, 0, 1),
        counts,
        couplings,
        coefficients.reshape(n_blocks, order, columns),
        beta_tiles,
    )


def solution(mesh):
    n_alpha, n_beta = mesh.shape["alpha"], mesh.shape["beta"]
    n_chips = n_alpha // 2
    rounds = n_chips.bit_length() - 1

    def per_device(coefficients, couplings, exc_list, counts, beta_tiles):
        order = couplings.shape[1]
        rows, columns = coefficients.shape
        n_blocks = rows // order
        n_stops = beta_tiles.shape[0]
        if n_beta == n_stops == 4:
            return line_call(mesh, coefficients, couplings, exc_list, counts, beta_tiles)
        widths, _ = split(columns)
        chunks = len(widths)
        vmem, smem = pl.BlockSpec(memory_space=pltpu.VMEM), pl.BlockSpec(memory_space=pltpu.SMEM)
        hbm = pl.BlockSpec(memory_space=pl.ANY)
        return pl.pallas_call(
            functools.partial(kernel, n_alpha, n_beta, rounds, chunks),
            out_shape=pltpu.VMEM((rows, columns), jnp.float32),
            in_specs=[smem, smem, vmem, hbm, hbm],
            out_specs=vmem,
            scratch_shapes=[
                pltpu.VMEM((rows, n_alpha * order), jnp.bfloat16),
                pltpu.VMEM((n_alpha * order, max(widths)), jnp.bfloat16),
                pltpu.VMEM(beta_tiles.shape, jnp.bfloat16),
                [pltpu.VMEM((n_alpha, n_blocks, order, width), jnp.bfloat16) for width in widths],
                [pltpu.VMEM((n_stops, rows, width), jnp.bfloat16) for width in widths],
                pltpu.SemaphoreType.DMA((chunks, n_alpha)),
                pltpu.SemaphoreType.DMA((chunks, n_alpha)),
                pltpu.SemaphoreType.DMA((chunks,)),
                pltpu.SemaphoreType.DMA((chunks, n_stops - 1)),
                pltpu.SemaphoreType.DMA((chunks, n_stops - 1)),
                pltpu.SemaphoreType.DMA(()),
            ],
            compiler_params=pltpu.CompilerParams(
                collective_id=0, has_side_effects=True, vmem_limit_bytes=48 * 2**20
            ),
        )(
            exc_list.transpose(2, 0, 1),
            counts,
            couplings,
            coefficients.reshape(n_blocks, order, columns),
            beta_tiles,
        )

    placed = (P("alpha", "beta"), P(), P(), P(), P(None, None, "beta"))
    return jax.shard_map(
        per_device, mesh=mesh, in_specs=placed, out_specs=P("alpha", "beta"), check_vma=False
    )
```

```python
import functools

import jax
import jax.numpy as jnp
from jax import lax
from jax.experimental import pallas as pl
from jax.experimental.pallas import tpu as pltpu
from jax.sharding import PartitionSpec as P

MESH = pl.DeviceIdType.MESH
WIDTHS = (1, 2, 2, 2, 1)
TILE = 256
AHEAD = 1
SHARES = (1, 1, 1, 1, 1, 1, 1, 1)
PIECES = 4
LANES = 128


def split(columns):
    unit = columns // sum(WIDTHS)
    widths = [unit * part for part in WIDTHS]
    return widths, [sum(widths[:c]) for c in range(len(widths))]


def flip(position, mask):
    bit = lax.rem(lax.div(position, mask), 2)
    return position + mask * (1 - 2 * bit)


def kernel(
    n_alpha, n_beta, rounds, chunks,
    exc_ref, counts_ref, coupling_ref, c_hbm, b_hbm, out_ref,
    weights, gathered, tiles, held, moved,
    send_sem, recv_sem, own_sem, zsend_sem, zrecv_sem, tile_sem,
):
    n_chips = n_alpha // 2
    n_blocks, order = c_hbm.shape[0], c_hbm.shape[1]
    n_stops = b_hbm.shape[0]
    widths, starts = split(out_ref.shape[1])
    alpha, beta = lax.axis_index("alpha"), lax.axis_index("beta")
    chip, core = lax.div(alpha, 2), lax.rem(alpha, 2)

    def mask_of(step, which):
        return (1 - which) * 2**step + which * 2 ** (rounds - 1 - step)

    def origin(label, which):
        source = chip
        for step in range(rounds):
            if (label >> step) & 1:
                source = flip(source, mask_of(step, which))
        return source * 2 + which

    if n_beta == n_stops:
        way, far, near = 1 - 2 * core, n_beta // 2, n_beta - 1 - n_beta // 2
    else:
        way, far, near = 1, n_stops - 1, 0
    ahead = lax.rem(beta + way + n_beta, n_beta)
    behind = lax.rem(beta - way + n_beta, n_beta)

    sibling = (alpha + 1 - 2 * core, beta)
    neighbours = [(flip(chip, mask_of(step, core)) * 2 + core, beta) for step in range(rounds)]
    greeted = neighbours + [sibling, (alpha, ahead), (alpha, behind)]
    barrier = pltpu.get_barrier_semaphore()
    for device in greeted:
        pl.semaphore_signal(barrier, inc=1, device_id=device, device_id_type=MESH)
    own = []
    for c in range(chunks):
        own.append(
            pltpu.make_async_copy(c_hbm.at[:, :, pl.ds(starts[c], widths[c])], held[c].at[0], own_sem.at[c])
        )
    own[0].start()
    pl.semaphore_wait(barrier, len(greeted))

    def to_alpha(c, label, target, device):
        source = c_hbm.at[:, :, pl.ds(starts[c], widths[c])] if label == 0 else held[c].at[label]
        return pltpu.make_async_remote_copy(
            src_ref=source,
            dst_ref=held[c].at[target],
            send_sem=send_sem.at[c, target],
            recv_sem=recv_sem.at[c, target],
            device_id=device,
            device_id_type=MESH,
        )

    copies = [{} for _ in range(chunks)]

    def pass_on(c, label):
        for step in range(label.bit_length(), rounds):
            target = label + 2**step
            copies[c][target] = to_alpha(c, label, target, neighbours[step])
            copies[c][target].start()
        target = n_chips + label
        copies[c][target] = to_alpha(c, label, target, sibling)
        copies[c][target].start()

    def slot_of(hop):
        return lax.rem(hop * way + n_beta * n_stops, n_beta)

    hops = [{} for _ in range(chunks)]

    def to_beta(c, kind, hop):
        sign, device, index = (1, ahead, hop - 1) if kind == "far" else (-1, behind, far + hop - 1)
        copy = pltpu.make_async_remote_copy(
            src_ref=moved[c].at[slot_of(sign * (hop - 1))],
            dst_ref=moved[c].at[slot_of(sign * hop)],
            send_sem=zsend_sem.at[c, index],
            recv_sem=zrecv_sem.at[c, index],
            device_id=(alpha, device),
            device_id_type=MESH,
        )
        hops[c][kind, hop] = copy
        copy.start()

    for c in range(min(AHEAD, chunks)):
        if c > 0:
            own[c].start()
        pass_on(c, 0)
    tile_copy = pltpu.make_async_copy(b_hbm, tiles, tile_sem)
    tile_copy.start()

    sources = [origin(label, core) for label in range(n_chips)]
    sources += [origin(label, 1 - core) for label in range(n_chips)]
    picked = []
    for slot, source in enumerate(sources):
        live = counts_ref[source, alpha] == 1
        picked.append(jnp.clip(exc_ref[0, source, alpha] - source * n_blocks, 0, n_blocks - 1))
        target = exc_ref[1, source, alpha] - alpha * n_blocks
        matrix = coupling_ref[exc_ref[2, source, alpha]]
        for block in range(n_blocks):
            keep = jnp.where(live & (target == block), 1.0, 0.0).astype(jnp.float32)
            weights[pl.ds(block * order, order), pl.ds(slot * order, order)] = (
                matrix.astype(jnp.float32) * keep
            ).astype(jnp.bfloat16)

    def product(c):
        @pl.loop(0, out_ref.shape[1] // TILE)
        def _(n):
            columns = pl.ds(pl.multiple_of(n * TILE, TILE), TILE)
            left = jnp.concatenate([moved[c][d] for d in range(n_stops)], axis=1)
            right = jnp.concatenate(
                [tiles[d, pl.ds(starts[c], widths[c]), columns] for d in range(n_stops)], axis=0
            )
            value = jnp.dot(left, right, preferred_element_type=jnp.float32)
            if c == 0:
                out_ref[:, columns] = value
            else:
                out_ref[:, columns] += value

    def relay(c):
        for kind, last in (("far", far), ("near", near)):
            for hop in range(1, last):
                hops[c][kind, hop].wait_recv()
                to_beta(c, kind, hop + 1)

    def finish(c):
        for kind, last in (("far", far), ("near", near)):
            if last > 0:
                hops[c][kind, last].wait_recv()
        if c == 0:
            tile_copy.wait()
        product(c)

    for c in range(chunks):
        for label in range(1, n_chips):
            copies[c][label].wait_recv()
            pass_on(c, label)
            if label == 1 and c + AHEAD < chunks:
                own[c + AHEAD].start()
                pass_on(c + AHEAD, 0)
        own[c].wait()
        for label in range(n_chips):
            copies[c][n_chips + label].wait_recv()
        for slot in range(n_alpha):
            gathered[pl.ds(slot * order, order), pl.ds(0, widths[c])] = held[c][slot, picked[slot]]
        moved[c][0] = jnp.dot(
            weights[...], gathered[:, pl.ds(0, widths[c])], preferred_element_type=jnp.float32
        ).astype(jnp.bfloat16)
        to_beta(c, "far", 1)
        if near > 0:
            to_beta(c, "near", 1)
        if c >= 1:
            relay(c - 1)
        if c >= 2:
            finish(c - 2)
    relay(chunks - 1)
    for c in range(max(chunks - 2, 0), chunks):
        finish(c)
    for c in range(chunks):
        for copy in copies[c].values():
            copy.wait_send()
        for copy in hops[c].values():
            copy.wait_send()


def line_kernel(
    n_alpha, n_beta, rounds, heights, early,
    exc_hbm, counts_hbm, coupling_hbm, c_hbm, b_hbm, out_ref,
    exc_ref, counts_ref, coupling_ref, weights, tiles, blocks, outer_tiles, partial, remote_sum, held, gathered,
    in_sem, raw_send, raw_recv, sum_send, sum_recv, tile_send, tile_recv, spread_send, spread_recv, send_sem, recv_sem,
):
    n_chips = n_alpha // 2
    n_blocks, order, columns = c_hbm.shape
    chunks = len(heights)
    offsets = [sum(heights[:c]) for c in range(chunks)]
    alpha, beta = lax.axis_index("alpha"), lax.axis_index("beta")
    chip, core = lax.div(alpha, 2), lax.rem(alpha, 2)
    side = lax.div(beta, 2)
    outer, inner = 3 * side, 1 + side
    across, beyond = 2 - side, 3 - 3 * side
    is_outer = beta == outer

    def mask_of(step, which):
        return (1 - which) * 2**step + which * 2 ** (rounds - 1 - step)

    def origin(label, which):
        source = chip
        for step in range(rounds):
            if (label >> step) & 1:
                source = flip(source, mask_of(step, which))
        return source * 2 + which

    def distance(source):
        return lax.rem(beta - source + n_beta, n_beta)

    sources = [origin(label, core) for label in range(n_chips)]
    sources += [origin(label, 1 - core) for label in range(n_chips)]
    sibling = (alpha + 1 - 2 * core, beta)
    neighbours = [(flip(chip, mask_of(step, core)) * 2 + core, beta) for step in range(rounds)]
    near = (alpha, is_outer.astype(jnp.int32) * inner + (1 - is_outer.astype(jnp.int32)) * outer)
    facing = (alpha, across)

    barrier = pltpu.get_barrier_semaphore()
    for device in neighbours + [sibling, near]:
        pl.semaphore_signal(barrier, inc=1, device_id=device, device_id_type=MESH)

    @pl.when(jnp.logical_not(is_outer))
    def _():
        pl.semaphore_signal(barrier, inc=1, device_id=facing, device_id_type=MESH)

    local = [
        pltpu.make_async_copy(exc_hbm, exc_ref, in_sem.at[0]),
        pltpu.make_async_copy(counts_hbm, counts_ref, in_sem.at[1]),
        pltpu.make_async_copy(coupling_hbm, coupling_ref, in_sem.at[2]),
        pltpu.make_async_copy(c_hbm, blocks.at[beta], in_sem.at[3]),
        pltpu.make_async_copy(b_hbm, tiles, in_sem.at[4]),
    ]
    for copy in local:
        copy.start()
    pl.semaphore_wait(barrier, rounds + 3 - is_outer.astype(jnp.int32))

    def rows_of(c):
        return pl.ds(offsets[c], heights[c])

    def remote(source, target, send, recv, device):
        return pltpu.make_async_remote_copy(
            src_ref=source, dst_ref=target, send_sem=send, recv_sem=recv, device_id=device, device_id_type=MESH
        )

    def raw(c, plane, kind, device):
        source = c_hbm.at[:, rows_of(c)] if kind < 2 else blocks.at[plane, :, rows_of(c)]
        return remote(
            source, blocks.at[plane, :, rows_of(c)], raw_send.at[kind, c], raw_recv.at[plane, c], device
        )

    def sum_copy(c):
        here = remote_sum.at[:, rows_of(c)]
        return remote(here, here, sum_send.at[c], sum_recv.at[c], near)

    piece = 2 * b_hbm.shape[1] // n_alpha
    part = piece // PIECES

    def tile_copy(q):
        row = alpha * piece + q * part
        which = lax.div(row, b_hbm.shape[1])
        tile = (1 - which) * 2 + which * (1 + 2 * side)
        source = b_hbm.at[tile, pl.ds(pl.multiple_of(lax.rem(row, b_hbm.shape[1]), part), part)]
        target = outer_tiles.at[pl.ds(pl.multiple_of(row, part), part)]
        return remote(source, target, tile_send.at[q], tile_recv.at[q], near)

    def tile_spread(q, label, target, device):
        here = outer_tiles.at[pl.ds(pl.multiple_of(sources[label] * piece + q * part, part), part)]
        return remote(here, here, spread_send.at[q, target], spread_recv.at[q, target], device)

    def held_spread(c, label, target, device):
        return remote(held[c].at[label], held[c].at[target], send_sem.at[c, target], recv_sem.at[c, target], device)

    def spread(make, index, label, sent):
        for step in range(label.bit_length(), rounds):
            sent.append(make(index, label, label + 2**step, neighbours[step]))
            sent[-1].start()
        sent.append(make(index, label, n_chips + label, sibling))
        sent[-1].start()

    def arrive(make, index, label):
        make(index, label, label, sibling).wait_recv()

    def tile_arrive(q, label):
        here = outer_tiles.at[pl.ds(pl.multiple_of(sources[label] * piece + q * part, part), part)]
        remote(here, here, spread_send.at[q, label], spread_recv.at[q, label], sibling).wait_recv()

    def set_weights():
        for copy in local[:3]:
            copy.wait()
        picked = []
        for slot, source in enumerate(sources):
            live = counts_ref[source, alpha] == 1
            picked.append(jnp.clip(exc_ref[0, source, alpha] - source * n_blocks, 0, n_blocks - 1))
            target = exc_ref[1, source, alpha] - alpha * n_blocks
            matrix = coupling_ref[exc_ref[2, source, alpha]]
            for block in range(n_blocks):
                keep = jnp.where(live & (target == block), 1.0, 0.0).astype(jnp.float32)
                value = (matrix.astype(jnp.float32) * keep).astype(jnp.bfloat16)
                for half in range(order // LANES):
                    weights[half, pl.ds(block * order, order), pl.ds(slot * LANES, LANES)] = value[
                        :, half * LANES : (half + 1) * LANES
                    ]
        return picked

    def product(c, terms, store):
        @pl.loop(0, columns // TILE)
        def _(n):
            at = pl.ds(pl.multiple_of(n * TILE, TILE), TILE)
            value = None
            for plane, right in terms:
                left = blocks[plane, :, rows_of(c)].reshape(n_blocks * heights[c], columns)
                term = jnp.dot(left, right(at), preferred_element_type=jnp.float32)
                value = term if value is None else value + term
            store(at, value)

    def own_tile(plane):
        return lambda at: tiles[distance(plane), :, at]

    def far_tile(k):
        return lambda at: outer_tiles[pl.ds(k * columns, columns), at]

    def store_held(c):
        def store(at, value):
            held[c][0, :, :, at] = value.astype(jnp.bfloat16).reshape(n_blocks, heights[c], TILE)
        return store

    def store_sum(c):
        def store(at, value):
            remote_sum[:, rows_of(c), at] = value.astype(jnp.bfloat16).reshape(n_blocks, heights[c], TILE)
        return store

    def store_partial(c):
        def store(at, value):
            partial[:, rows_of(c), at] = value.reshape(n_blocks, heights[c], TILE)
        return store

    def relay(c, label):
        arrive(held_spread, c, label)
        spread(held_spread, c, label, sent)

    def finish(c, picked):
        for label in range(n_chips):
            arrive(held_spread, c, n_chips + label)
        half, within = offsets[c] // LANES, offsets[c] % LANES
        for slot in range(n_alpha):
            gathered[half, pl.ds(slot * LANES + within, heights[c])] = held[c][slot, picked[slot]]
        if within + heights[c] == LANES:
            @pl.loop(0, columns // TILE)
            def _(n):
                at = pl.ds(pl.multiple_of(n * TILE, TILE), TILE)
                value = jnp.dot(weights[half], gathered[half, :, at], preferred_element_type=jnp.float32)
                if half == 0:
                    out_ref[:, at] = value
                else:
                    out_ref[:, at] += value

    def follow(c, picked):
        for label in range(1, n_chips):
            behind = c - label.bit_count()
            if 0 <= behind < chunks:
                relay(behind, label)
        if 0 <= c - rounds - 1 < chunks:
            finish(c - rounds - 1, picked)

    def end(picked):
        for c in range(chunks, chunks + rounds + 1):
            follow(c, picked)
        for copy in sent:
            copy.wait_send()

    sent = []

    def start(copy):
        sent.append(copy)
        copy.start()

    @pl.when(is_outer)
    def _():
        for q in range(PIECES):
            start(tile_copy(q))
        for c in range(chunks):
            start(raw(c, outer, 0, near))
        picked = set_weights()
        local[3].wait()
        local[4].wait()
        for c in range(chunks):
            raw(c, inner, 0, near).wait_recv()
            product(c, [(outer, own_tile(outer)), (inner, own_tile(inner))], store_partial(c))
        for c in range(chunks):
            sum_copy(c).wait_recv()
            held[c][0] = (
                partial[:, rows_of(c)] + remote_sum[:, rows_of(c)].astype(jnp.float32)
            ).astype(jnp.bfloat16)
            spread(held_spread, c, 0, sent)
            follow(c, picked)
        end(picked)

    sent = []

    @pl.when(jnp.logical_not(is_outer))
    def _():
        for c in range(chunks):
            start(raw(c, inner, 0, near))
        for c in range(early):
            start(raw(c, inner, 1, facing))
        picked = set_weights()
        def tile_follow(q):
            for label in range(1, n_chips):
                behind = q - label.bit_count()
                if 0 <= behind < PIECES:
                    tile_arrive(behind, label)
                    spread(tile_spread, behind, label, sent)

        def pass_on(c):
            if c < chunks:
                raw(c, outer, 0, near).wait_recv()
                start(raw(c, outer, 2, facing))
                if c >= 1 and c - 1 + early < chunks:
                    start(raw(c - 1 + early, inner, 1, facing))

        for q in range(PIECES):
            tile_copy(q).wait_recv()
            spread(tile_spread, q, 0, sent)
            tile_follow(q)
        pass_on(0)
        tile_follow(PIECES)
        pass_on(1)
        for q in range(PIECES + 1, PIECES + rounds):
            tile_follow(q)
        pass_on(2)
        local[3].wait()
        local[4].wait()
        for q in range(PIECES):
            for label in range(n_chips):
                tile_arrive(q, n_chips + label)
        for c in range(chunks):
            raw(c, across, 1, facing).wait_recv()
            raw(c, beyond, 2, facing).wait_recv()
            product(c, [(across, far_tile(0)), (beyond, far_tile(1))], store_sum(c))
            start(sum_copy(c))
            product(c, [(plane, own_tile(plane)) for plane in (inner, outer, across, beyond)], store_held(c))
            spread(held_spread, c, 0, sent)
            follow(c, picked)
            pass_on(c + 3)
        end(picked)


def line_call(mesh, coefficients, couplings, exc_list, counts, beta_tiles):
    n_alpha, n_beta = mesh.shape["alpha"], mesh.shape["beta"]
    order = couplings.shape[1]
    rows, columns = coefficients.shape
    n_blocks = rows // order
    heights = [order * share // sum(SHARES) for share in SHARES]
    chunks = len(heights)
    hbm = pl.BlockSpec(memory_space=pl.ANY)
    dma = pltpu.SemaphoreType.DMA
    return pl.pallas_call(
        functools.partial(line_kernel, n_alpha, n_beta, (n_alpha // 2).bit_length() - 1, heights, 6),
        out_shape=pltpu.VMEM((rows, columns), jnp.float32),
        in_specs=[hbm] * 5,
        out_specs=pl.BlockSpec(memory_space=pltpu.VMEM),
        scratch_shapes=[
            pltpu.SMEM((3, n_alpha, n_alpha), jnp.int32),
            pltpu.SMEM((n_alpha, n_alpha), jnp.int32),
            pltpu.VMEM(couplings.shape, jnp.bfloat16),
            pltpu.VMEM((order // LANES, rows, n_alpha * LANES), jnp.bfloat16),
            pltpu.VMEM(beta_tiles.shape, jnp.bfloat16),
            pltpu.VMEM((n_beta, n_blocks, order, columns), jnp.bfloat16),
            pltpu.VMEM((2 * columns, columns), jnp.bfloat16),
            pltpu.VMEM((n_blocks, order, columns), jnp.float32),
            pltpu.VMEM((n_blocks, order, columns), jnp.bfloat16),
            [pltpu.VMEM((n_alpha, n_blocks, height, columns), jnp.bfloat16) for height in heights],
            pltpu.VMEM((order // LANES, n_alpha * LANES, columns), jnp.bfloat16),
            dma((5,)),
            dma((3, chunks)),
            dma((n_beta, chunks)),
            dma((chunks,)),
            dma((chunks,)),
            dma((PIECES,)),
            dma((PIECES,)),
            dma((PIECES, n_alpha)),
            dma((PIECES, n_alpha)),
            dma((chunks, n_alpha)),
            dma((chunks, n_alpha)),
        ],
        compiler_params=pltpu.CompilerParams(
            collective_id=0, has_side_effects=True, vmem_limit_bytes=60 * 2**20
        ),
    )(
        exc_list.transpose(2, 0, 1),
        counts,
        couplings,
        coefficients.reshape(n_blocks, order, columns),
        beta_tiles,
    )


def solution(mesh):
    n_alpha, n_beta = mesh.shape["alpha"], mesh.shape["beta"]
    n_chips = n_alpha // 2
    rounds = n_chips.bit_length() - 1

    def per_device(coefficients, couplings, exc_list, counts, beta_tiles):
        order = couplings.shape[1]
        rows, columns = coefficients.shape
        n_blocks = rows // order
        n_stops = beta_tiles.shape[0]
        if n_beta == n_stops == 4:
            return line_call(mesh, coefficients, couplings, exc_list, counts, beta_tiles)
        widths, _ = split(columns)
        chunks = len(widths)
        vmem, smem = pl.BlockSpec(memory_space=pltpu.VMEM), pl.BlockSpec(memory_space=pltpu.SMEM)
        hbm = pl.BlockSpec(memory_space=pl.ANY)
        return pl.pallas_call(
            functools.partial(kernel, n_alpha, n_beta, rounds, chunks),
            out_shape=pltpu.VMEM((rows, columns), jnp.float32),
            in_specs=[smem, smem, vmem, hbm, hbm],
            out_specs=vmem,
            scratch_shapes=[
                pltpu.VMEM((rows, n_alpha * order), jnp.bfloat16),
                pltpu.VMEM((n_alpha * order, max(widths)), jnp.bfloat16),
                pltpu.VMEM(beta_tiles.shape, jnp.bfloat16),
                [pltpu.VMEM((n_alpha, n_blocks, order, width), jnp.bfloat16) for width in widths],
                [pltpu.VMEM((n_stops, rows, width), jnp.bfloat16) for width in widths],
                pltpu.SemaphoreType.DMA((chunks, n_alpha)),
                pltpu.SemaphoreType.DMA((chunks, n_alpha)),
                pltpu.SemaphoreType.DMA((chunks,)),
                pltpu.SemaphoreType.DMA((chunks, n_stops - 1)),
                pltpu.SemaphoreType.DMA((chunks, n_stops - 1)),
                pltpu.SemaphoreType.DMA(()),
            ],
            compiler_params=pltpu.CompilerParams(
                collective_id=0, has_side_effects=True, vmem_limit_bytes=48 * 2**20
            ),
        )(
            exc_list.transpose(2, 0, 1),
            counts,
            couplings,
            coefficients.reshape(n_blocks, order, columns),
            beta_tiles,
        )

    placed = (P("alpha", "beta"), P(), P(), P(), P(None, None, "beta"))
    return jax.shard_map(
        per_device, mesh=mesh, in_specs=placed, out_specs=P("alpha", "beta"), check_vma=False
    )
```

```python
import functools

import jax
import jax.numpy as jnp
from jax import lax
from jax.experimental import pallas as pl
from jax.experimental.pallas import tpu as pltpu
from jax.sharding import PartitionSpec as P

MESH = pl.DeviceIdType.MESH
WIDTHS = (1, 2, 2, 2, 1)
TILE = 256
AHEAD = 1
SHARES = (1, 1, 1, 1, 1, 1, 1, 1)
PIECES = 4
LAG = 2
RAW = 2
FIRST = 4
SECOND = 6
LANES = 128


def split(columns):
    unit = columns // sum(WIDTHS)
    widths = [unit * part for part in WIDTHS]
    return widths, [sum(widths[:c]) for c in range(len(widths))]


def flip(position, mask):
    bit = lax.rem(lax.div(position, mask), 2)
    return position + mask * (1 - 2 * bit)


def kernel(
    n_alpha, n_beta, rounds, chunks,
    exc_ref, counts_ref, coupling_ref, c_hbm, b_hbm, out_ref,
    weights, gathered, tiles, held, moved,
    send_sem, recv_sem, own_sem, zsend_sem, zrecv_sem, tile_sem,
):
    n_chips = n_alpha // 2
    n_blocks, order = c_hbm.shape[0], c_hbm.shape[1]
    n_stops = b_hbm.shape[0]
    widths, starts = split(out_ref.shape[1])
    alpha, beta = lax.axis_index("alpha"), lax.axis_index("beta")
    chip, core = lax.div(alpha, 2), lax.rem(alpha, 2)

    def mask_of(step, which):
        return (1 - which) * 2**step + which * 2 ** (rounds - 1 - step)

    def origin(label, which):
        source = chip
        for step in range(rounds):
            if (label >> step) & 1:
                source = flip(source, mask_of(step, which))
        return source * 2 + which

    if n_beta == n_stops:
        way, far, near = 1 - 2 * core, n_beta // 2, n_beta - 1 - n_beta // 2
    else:
        way, far, near = 1, n_stops - 1, 0
    ahead = lax.rem(beta + way + n_beta, n_beta)
    behind = lax.rem(beta - way + n_beta, n_beta)

    sibling = (alpha + 1 - 2 * core, beta)
    neighbours = [(flip(chip, mask_of(step, core)) * 2 + core, beta) for step in range(rounds)]
    greeted = neighbours + [sibling, (alpha, ahead), (alpha, behind)]
    barrier = pltpu.get_barrier_semaphore()
    for device in greeted:
        pl.semaphore_signal(barrier, inc=1, device_id=device, device_id_type=MESH)
    own = []
    for c in range(chunks):
        own.append(
            pltpu.make_async_copy(c_hbm.at[:, :, pl.ds(starts[c], widths[c])], held[c].at[0], own_sem.at[c])
        )
    own[0].start()
    pl.semaphore_wait(barrier, len(greeted))

    def to_alpha(c, label, target, device):
        source = c_hbm.at[:, :, pl.ds(starts[c], widths[c])] if label == 0 else held[c].at[label]
        return pltpu.make_async_remote_copy(
            src_ref=source,
            dst_ref=held[c].at[target],
            send_sem=send_sem.at[c, target],
            recv_sem=recv_sem.at[c, target],
            device_id=device,
            device_id_type=MESH,
        )

    copies = [{} for _ in range(chunks)]

    def pass_on(c, label):
        for step in range(label.bit_length(), rounds):
            target = label + 2**step
            copies[c][target] = to_alpha(c, label, target, neighbours[step])
            copies[c][target].start()
        target = n_chips + label
        copies[c][target] = to_alpha(c, label, target, sibling)
        copies[c][target].start()

    def slot_of(hop):
        return lax.rem(hop * way + n_beta * n_stops, n_beta)

    hops = [{} for _ in range(chunks)]

    def to_beta(c, kind, hop):
        sign, device, index = (1, ahead, hop - 1) if kind == "far" else (-1, behind, far + hop - 1)
        copy = pltpu.make_async_remote_copy(
            src_ref=moved[c].at[slot_of(sign * (hop - 1))],
            dst_ref=moved[c].at[slot_of(sign * hop)],
            send_sem=zsend_sem.at[c, index],
            recv_sem=zrecv_sem.at[c, index],
            device_id=(alpha, device),
            device_id_type=MESH,
        )
        hops[c][kind, hop] = copy
        copy.start()

    for c in range(min(AHEAD, chunks)):
        if c > 0:
            own[c].start()
        pass_on(c, 0)
    tile_copy = pltpu.make_async_copy(b_hbm, tiles, tile_sem)
    tile_copy.start()

    sources = [origin(label, core) for label in range(n_chips)]
    sources += [origin(label, 1 - core) for label in range(n_chips)]
    picked = []
    for slot, source in enumerate(sources):
        live = counts_ref[source, alpha] == 1
        picked.append(jnp.clip(exc_ref[0, source, alpha] - source * n_blocks, 0, n_blocks - 1))
        target = exc_ref[1, source, alpha] - alpha * n_blocks
        matrix = coupling_ref[exc_ref[2, source, alpha]]
        for block in range(n_blocks):
            keep = jnp.where(live & (target == block), 1.0, 0.0).astype(jnp.float32)
            weights[pl.ds(block * order, order), pl.ds(slot * order, order)] = (
                matrix.astype(jnp.float32) * keep
            ).astype(jnp.bfloat16)

    def product(c):
        @pl.loop(0, out_ref.shape[1] // TILE)
        def _(n):
            columns = pl.ds(pl.multiple_of(n * TILE, TILE), TILE)
            left = jnp.concatenate([moved[c][d] for d in range(n_stops)], axis=1)
            right = jnp.concatenate(
                [tiles[d, pl.ds(starts[c], widths[c]), columns] for d in range(n_stops)], axis=0
            )
            value = jnp.dot(left, right, preferred_element_type=jnp.float32)
            if c == 0:
                out_ref[:, columns] = value
            else:
                out_ref[:, columns] += value

    def relay(c):
        for kind, last in (("far", far), ("near", near)):
            for hop in range(1, last):
                hops[c][kind, hop].wait_recv()
                to_beta(c, kind, hop + 1)

    def finish(c):
        for kind, last in (("far", far), ("near", near)):
            if last > 0:
                hops[c][kind, last].wait_recv()
        if c == 0:
            tile_copy.wait()
        product(c)

    for c in range(chunks):
        for label in range(1, n_chips):
            copies[c][label].wait_recv()
            pass_on(c, label)
            if label == 1 and c + AHEAD < chunks:
                own[c + AHEAD].start()
                pass_on(c + AHEAD, 0)
        own[c].wait()
        for label in range(n_chips):
            copies[c][n_chips + label].wait_recv()
        for slot in range(n_alpha):
            gathered[pl.ds(slot * order, order), pl.ds(0, widths[c])] = held[c][slot, picked[slot]]
        moved[c][0] = jnp.dot(
            weights[...], gathered[:, pl.ds(0, widths[c])], preferred_element_type=jnp.float32
        ).astype(jnp.bfloat16)
        to_beta(c, "far", 1)
        if near > 0:
            to_beta(c, "near", 1)
        if c >= 1:
            relay(c - 1)
        if c >= 2:
            finish(c - 2)
    relay(chunks - 1)
    for c in range(max(chunks - 2, 0), chunks):
        finish(c)
    for c in range(chunks):
        for copy in copies[c].values():
            copy.wait_send()
        for copy in hops[c].values():
            copy.wait_send()


def line_kernel(
    n_alpha, n_beta, rounds, heights,
    exc_hbm, counts_hbm, coupling_hbm, c_hbm, b_hbm, out_ref,
    exc_ref, counts_ref, coupling_ref, weights, tiles, blocks, outer_tiles, partial, remote_sum, held, gathered,
    in_sem, raw_send, raw_recv, sum_send, sum_recv, tile_send, tile_recv, spread_send, spread_recv, spread_last,
    send_sem, recv_sem,
):
    n_chips = n_alpha // 2
    n_blocks, order, columns = c_hbm.shape
    chunks = len(heights)
    offsets = [sum(heights[:c]) for c in range(chunks)]
    alpha, beta = lax.axis_index("alpha"), lax.axis_index("beta")
    chip, core = lax.div(alpha, 2), lax.rem(alpha, 2)
    side = lax.div(beta, 2)
    outer, inner = 3 * side, 1 + side
    across, beyond = 2 - side, 3 - 3 * side
    is_outer = beta == outer

    def mask_of(step, which):
        return (1 - which) * 2**step + which * 2 ** (rounds - 1 - step)

    def origin(label, which):
        source = chip
        for step in range(rounds):
            if (label >> step) & 1:
                source = flip(source, mask_of(step, which))
        return source * 2 + which

    def distance(source):
        return lax.rem(beta - source + n_beta, n_beta)

    sources = [origin(label, core) for label in range(n_chips)]
    sources += [origin(label, 1 - core) for label in range(n_chips)]
    sibling = (alpha + 1 - 2 * core, beta)
    neighbours = [(flip(chip, mask_of(step, core)) * 2 + core, beta) for step in range(rounds)]
    near = (alpha, is_outer.astype(jnp.int32) * inner + (1 - is_outer.astype(jnp.int32)) * outer)
    facing = (alpha, across)

    barrier = pltpu.get_barrier_semaphore()
    for device in neighbours + [sibling, near]:
        pl.semaphore_signal(barrier, inc=1, device_id=device, device_id_type=MESH)

    @pl.when(jnp.logical_not(is_outer))
    def _():
        pl.semaphore_signal(barrier, inc=1, device_id=facing, device_id_type=MESH)

    local = [
        pltpu.make_async_copy(exc_hbm, exc_ref, in_sem.at[0]),
        pltpu.make_async_copy(counts_hbm, counts_ref, in_sem.at[1]),
        pltpu.make_async_copy(coupling_hbm, coupling_ref, in_sem.at[2]),
        pltpu.make_async_copy(c_hbm, blocks.at[beta], in_sem.at[3]),
        pltpu.make_async_copy(b_hbm, tiles, in_sem.at[4]),
    ]
    for copy in local:
        copy.start()
    pl.semaphore_wait(barrier, rounds + 3 - is_outer.astype(jnp.int32))

    def rows_of(c):
        return pl.ds(offsets[c], heights[c])

    def remote(source, target, send, recv, device):
        return pltpu.make_async_remote_copy(
            src_ref=source, dst_ref=target, send_sem=send, recv_sem=recv, device_id=device, device_id_type=MESH
        )

    def raw(c, plane, kind, device):
        source = c_hbm.at[:, rows_of(c)] if kind < 2 else blocks.at[plane, :, rows_of(c)]
        return remote(source, blocks.at[plane, :, rows_of(c)], raw_send.at[kind], raw_recv.at[plane, c], device)

    def sum_copy(c):
        here = remote_sum.at[:, rows_of(c)]
        return remote(here, here, sum_send, sum_recv.at[c], near)

    piece = 2 * b_hbm.shape[1] // n_alpha
    part = piece // PIECES

    def part_of(label, q):
        return pl.ds(pl.multiple_of(sources[label] * piece + q * part, part), part)

    def tile_copy(q):
        row = alpha * piece + q * part
        which = lax.div(row, b_hbm.shape[1])
        tile = (1 - which) * 2 + which * (1 + 2 * side)
        source = b_hbm.at[tile, pl.ds(pl.multiple_of(lax.rem(row, b_hbm.shape[1]), part), part)]
        return remote(source, outer_tiles.at[part_of(0, q)], tile_send, tile_recv.at[q], near)

    def group_of(label):
        return label.bit_count() - 1 if label < n_chips else rounds

    def tile_spread(q, label, target, device):
        here = outer_tiles.at[part_of(label, q)]
        recv = spread_recv.at[q, group_of(target)] if target < n_chips else spread_last
        return remote(here, here, spread_send, recv, device)

    def held_spread(c, label, target, device):
        return remote(
            held[c].at[label], held[c].at[target], send_sem.at[c], recv_sem.at[c, group_of(target)], device
        )

    def spread(make, index, label):
        for step in range(label.bit_length(), rounds):
            make(index, label, label + 2**step, neighbours[step]).start()
        make(index, label, n_chips + label, sibling).start()

    labels_of = [range(1, n_chips - 1), range(n_chips - 1, n_chips), range(n_chips, n_alpha)]

    def tile_relay(q, group):
        count = len(labels_of[group]) * part
        here = outer_tiles.at[pl.ds(0, count)]
        remote(here, here, spread_send, spread_recv.at[q, group], sibling).wait_recv()
        for label in labels_of[group]:
            spread(tile_spread, q, label)

    def held_arrive(c, group):
        labels = labels_of[group]
        here = held[c].at[pl.ds(labels[0], len(labels))]
        remote(here, here, send_sem.at[c], recv_sem.at[c, group], sibling).wait_recv()

    def set_weights():
        for copy in local[:3]:
            copy.wait()
        picked = []
        for slot, source in enumerate(sources):
            live = counts_ref[source, alpha] == 1
            picked.append(jnp.clip(exc_ref[0, source, alpha] - source * n_blocks, 0, n_blocks - 1))
            target = exc_ref[1, source, alpha] - alpha * n_blocks
            matrix = coupling_ref[exc_ref[2, source, alpha]]
            for block in range(n_blocks):
                keep = jnp.where(live & (target == block), 1.0, 0.0).astype(jnp.float32)
                value = (matrix.astype(jnp.float32) * keep).astype(jnp.bfloat16)
                for half in range(order // LANES):
                    weights[half, pl.ds(block * order, order), pl.ds(slot * LANES, LANES)] = value[
                        :, half * LANES : (half + 1) * LANES
                    ]
        return picked

    def product(first, count, planes, tile, store, before=False):
        at_rows = pl.ds(offsets[first], sum(heights[first : first + count]))

        @pl.loop(0, columns // TILE)
        def _(n):
            at = pl.ds(pl.multiple_of(n * TILE, TILE), TILE)
            value = None
            for k, plane in enumerate(planes):
                left = blocks[plane, :, at_rows].reshape(n_blocks * at_rows.size, columns)
                term = jnp.dot(left, tile(k, plane, at), preferred_element_type=jnp.float32)
                value = term if value is None else value + term
            value = value.reshape(n_blocks, at_rows.size, TILE)
            if before:
                value = value + partial[:, at_rows, at]
            store(at_rows, at, value)

    def own_tile(k, plane, at):
        return tiles[distance(plane), :, at]

    def far_tile(k, plane, at):
        return outer_tiles[pl.ds(k * columns, columns), at]

    def store_held(c):
        def store(at_rows, at, value):
            held[c][0, :, :, at] = value.astype(jnp.bfloat16)
        return store

    def store_sum(at_rows, at, value):
        remote_sum[:, at_rows, at] = value.astype(jnp.bfloat16)

    def store_partial(at_rows, at, value):
        partial[:, at_rows, at] = value

    def relay(c, group):
        held_arrive(c, group)
        for label in labels_of[group]:
            spread(held_spread, c, label)

    def finish(c, picked):
        held_arrive(c, rounds)
        half, within = offsets[c] // LANES, offsets[c] % LANES
        for slot in range(n_alpha):
            gathered[half, pl.ds(slot * LANES + within, heights[c])] = held[c][slot, picked[slot]]
        if within + heights[c] == LANES:
            @pl.loop(0, columns // TILE)
            def _(n):
                at = pl.ds(pl.multiple_of(n * TILE, TILE), TILE)
                value = jnp.dot(weights[half], gathered[half, :, at], preferred_element_type=jnp.float32)
                if half == 0:
                    out_ref[:, at] = value
                else:
                    out_ref[:, at] += value

    def follow(c, picked):
        for group in range(rounds):
            behind = c - LAG * (group + 1)
            if 0 <= behind < chunks:
                relay(behind, group)
        if 0 <= c - LAG * rounds - 1 < chunks:
            finish(c - LAG * rounds - 1, picked)

    def end(picked):
        for c in range(chunks, chunks + LAG * rounds + 1):
            follow(c, picked)
        for c in range(chunks):
            here = held[c].at[pl.ds(1, n_alpha - 1)]
            remote(here, here, send_sem.at[c], recv_sem.at[c, 0], sibling).wait_send()

    def sent(ref, sem):
        remote(ref, ref, sem, sum_recv.at[0], near).wait_send()

    @pl.when(is_outer)
    def _():
        def own(c):
            raw(c, outer, 0, near).start()

        tile_copy(0).start()
        tile_copy(1).start()
        own(0)
        for q in range(2, PIECES):
            tile_copy(q).start()
        for c in range(1, chunks):
            own(c)
        picked = set_weights()
        local[3].wait()
        local[4].wait()

        def prepare(c):
            for k in range(c, c + 2):
                raw(k, inner, 0, near).wait_recv()
            product(c, 2, (outer, inner), own_tile, store_partial)

        def finish_raw(c):
            raw(c, across, 0, near).wait_recv()
            raw(c, beyond, 0, near).wait_recv()
            product(c, 1, (across, beyond), own_tile, store_held(c), before=True)
            spread(held_spread, c, 0)

        prepare(0)
        prepare(2)
        finish_raw(0)
        prepare(4)
        finish_raw(1)
        for c in range(RAW, chunks):
            sum_copy(c).wait_recv()
            if c == 6:
                prepare(6)
            held[c][0] = (
                partial[:, rows_of(c)] + remote_sum[:, rows_of(c)].astype(jnp.float32)
            ).astype(jnp.bfloat16)
            spread(held_spread, c, 0)
            follow(c, picked)
        end(picked)
        sent(outer_tiles.at[pl.ds(0, piece)], tile_send)
        sent(blocks.at[outer], raw_send.at[0])

    @pl.when(jnp.logical_not(is_outer))
    def _():
        def own_near(c):
            raw(c, inner, 0, near).start()

        def own_facing(c):
            raw(c, inner, 1, facing).start()

        for c in range(FIRST):
            own_near(c)
            own_facing(c)
        own_near(FIRST)
        picked = set_weights()
        local[3].wait()
        local[4].wait()

        def prepare(c):
            for k in range(c, c + 2):
                raw(k, across, 1, facing).wait_recv()
            product(c, 2, (inner, across), own_tile, store_partial)

        def pass_on(c):
            if c < chunks:
                raw(c, outer, 0, near).wait_recv()
                if c >= SECOND:
                    own_facing(c)
                raw(c, outer, 2, facing).start()

        def tile_own(q):
            tile_copy(q).wait_recv()
            spread(tile_spread, q, 0)

        def finish_held(c):
            product(c, 1, (outer, beyond), own_tile, store_held(c), before=True)
            spread(held_spread, c, 0)

        def send_beyond(c):
            raw(c, beyond, 2, facing).wait_recv()
            raw(c, beyond, 3, near).start()

        tile_own(0)
        tile_own(1)
        prepare(0)
        for c in range(RAW):
            raw(c, across, 3, near).start()
        pass_on(0)
        for c in range(FIRST, SECOND):
            own_facing(c)
        tile_relay(0, 0)
        tile_own(2)
        tile_relay(1, 0)
        prepare(2)
        tile_own(3)
        tile_relay(0, 1)
        send_beyond(0)
        for c in range(FIRST + 1, SECOND + 1):
            own_near(c)
        tile_relay(2, 0)
        pass_on(1)
        tile_relay(1, 1)
        tile_relay(3, 0)
        pass_on(2)
        finish_held(0)
        tile_relay(2, 1)
        prepare(4)
        pass_on(3)
        tile_relay(3, 1)
        send_beyond(1)
        finish_held(1)
        here = outer_tiles.at[pl.ds(0, n_chips * piece)]
        remote(here, here, spread_send, spread_last, sibling).wait_recv()
        for c in range(RAW, chunks):
            if c >= SECOND:
                raw(c, across, 1, facing).wait_recv()
            raw(c, beyond, 2, facing).wait_recv()
            product(c, 1, (across, beyond), far_tile, store_sum)
            sum_copy(c).start()
            if c == RAW + 1:
                own_near(chunks - 1)
            pass_on(c + 2)
            if c >= SECOND:
                product(c, 1, (inner, across), own_tile, store_partial)
            finish_held(c)
            follow(c, picked)
        end(picked)
        sent(outer_tiles.at[pl.ds(0, (n_alpha - 1) * piece)], spread_send)
        sent(remote_sum.at[:, pl.ds(offsets[RAW], order - offsets[RAW])], sum_send)
        for kind in range(3):
            sent(blocks.at[inner], raw_send.at[kind])
        sent(blocks.at[inner, :, pl.ds(0, offsets[2 * RAW])], raw_send.at[3])


def line_call(mesh, coefficients, couplings, exc_list, counts, beta_tiles):
    n_alpha, n_beta = mesh.shape["alpha"], mesh.shape["beta"]
    order = couplings.shape[1]
    rows, columns = coefficients.shape
    n_blocks = rows // order
    heights = [order * share // sum(SHARES) for share in SHARES]
    chunks = len(heights)
    rounds = (n_alpha // 2).bit_length() - 1
    hbm = pl.BlockSpec(memory_space=pl.ANY)
    dma = pltpu.SemaphoreType.DMA
    return pl.pallas_call(
        functools.partial(line_kernel, n_alpha, n_beta, rounds, heights),
        out_shape=pltpu.VMEM((rows, columns), jnp.float32),
        in_specs=[hbm] * 5,
        out_specs=pl.BlockSpec(memory_space=pltpu.VMEM),
        scratch_shapes=[
            pltpu.SMEM((3, n_alpha, n_alpha), jnp.int32),
            pltpu.SMEM((n_alpha, n_alpha), jnp.int32),
            pltpu.VMEM(couplings.shape, jnp.bfloat16),
            pltpu.VMEM((order // LANES, rows, n_alpha * LANES), jnp.bfloat16),
            pltpu.VMEM(beta_tiles.shape, jnp.bfloat16),
            pltpu.VMEM((n_beta, n_blocks, order, columns), jnp.bfloat16),
            pltpu.VMEM((2 * columns, columns), jnp.bfloat16),
            pltpu.VMEM((n_blocks, order, columns), jnp.float32),
            pltpu.VMEM((n_blocks, order, columns), jnp.bfloat16),
            [pltpu.VMEM((n_alpha, n_blocks, height, columns), jnp.bfloat16) for height in heights],
            pltpu.VMEM((order // LANES, n_alpha * LANES, columns), jnp.bfloat16),
            dma((5,)),
            dma((4,)),
            dma((n_beta, chunks)),
            dma(()),
            dma((chunks,)),
            dma(()),
            dma((PIECES,)),
            dma(()),
            dma((PIECES, rounds)),
            dma(()),
            dma((chunks,)),
            dma((chunks, rounds + 1)),
        ],
        compiler_params=pltpu.CompilerParams(
            collective_id=0, has_side_effects=True, vmem_limit_bytes=60 * 2**20
        ),
    )(
        exc_list.transpose(2, 0, 1),
        counts,
        couplings,
        coefficients.reshape(n_blocks, order, columns),
        beta_tiles,
    )


def solution(mesh):
    n_alpha, n_beta = mesh.shape["alpha"], mesh.shape["beta"]
    n_chips = n_alpha // 2
    rounds = n_chips.bit_length() - 1

    def per_device(coefficients, couplings, exc_list, counts, beta_tiles):
        order = couplings.shape[1]
        rows, columns = coefficients.shape
        n_blocks = rows // order
        n_stops = beta_tiles.shape[0]
        if n_alpha == 8 and n_beta == n_stops == 4:
            return line_call(mesh, coefficients, couplings, exc_list, counts, beta_tiles)
        widths, _ = split(columns)
        chunks = len(widths)
        vmem, smem = pl.BlockSpec(memory_space=pltpu.VMEM), pl.BlockSpec(memory_space=pltpu.SMEM)
        hbm = pl.BlockSpec(memory_space=pl.ANY)
        return pl.pallas_call(
            functools.partial(kernel, n_alpha, n_beta, rounds, chunks),
            out_shape=pltpu.VMEM((rows, columns), jnp.float32),
            in_specs=[smem, smem, vmem, hbm, hbm],
            out_specs=vmem,
            scratch_shapes=[
                pltpu.VMEM((rows, n_alpha * order), jnp.bfloat16),
                pltpu.VMEM((n_alpha * order, max(widths)), jnp.bfloat16),
                pltpu.VMEM(beta_tiles.shape, jnp.bfloat16),
                [pltpu.VMEM((n_alpha, n_blocks, order, width), jnp.bfloat16) for width in widths],
                [pltpu.VMEM((n_stops, rows, width), jnp.bfloat16) for width in widths],
                pltpu.SemaphoreType.DMA((chunks, n_alpha)),
                pltpu.SemaphoreType.DMA((chunks, n_alpha)),
                pltpu.SemaphoreType.DMA((chunks,)),
                pltpu.SemaphoreType.DMA((chunks, n_stops - 1)),
                pltpu.SemaphoreType.DMA((chunks, n_stops - 1)),
                pltpu.SemaphoreType.DMA(()),
            ],
            compiler_params=pltpu.CompilerParams(
                collective_id=0, has_side_effects=True, vmem_limit_bytes=48 * 2**20
            ),
        )(
            exc_list.transpose(2, 0, 1),
            counts,
            couplings,
            coefficients.reshape(n_blocks, order, columns),
            beta_tiles,
        )

    placed = (P("alpha", "beta"), P(), P(), P(), P(None, None, "beta"))
    return jax.shard_map(
        per_device, mesh=mesh, in_specs=placed, out_specs=P("alpha", "beta"), check_vma=False
    )
```

```python
import functools

import jax
import jax.numpy as jnp
from jax import lax
from jax.experimental import pallas as pl
from jax.experimental.pallas import tpu as pltpu
from jax.sharding import PartitionSpec as P

MESH = pl.DeviceIdType.MESH
WIDTHS = (1, 2, 2, 2, 1)
TILE = 256
AHEAD = 1
SHARES = (1, 1, 1, 1, 1, 1, 1, 1)
PIECES = 4
LAG = 2
RAW = 2
FIRST = 4
SECOND = 6
LANES = 64


def split(columns):
    unit = columns // sum(WIDTHS)
    widths = [unit * part for part in WIDTHS]
    return widths, [sum(widths[:c]) for c in range(len(widths))]


def flip(position, mask):
    bit = lax.rem(lax.div(position, mask), 2)
    return position + mask * (1 - 2 * bit)


def kernel(
    n_alpha, n_beta, rounds, chunks,
    exc_ref, counts_ref, coupling_ref, c_hbm, b_hbm, out_ref,
    weights, gathered, tiles, held, moved,
    send_sem, recv_sem, own_sem, zsend_sem, zrecv_sem, tile_sem,
):
    n_chips = n_alpha // 2
    n_blocks, order = c_hbm.shape[0], c_hbm.shape[1]
    n_stops = b_hbm.shape[0]
    widths, starts = split(out_ref.shape[1])
    alpha, beta = lax.axis_index("alpha"), lax.axis_index("beta")
    chip, core = lax.div(alpha, 2), lax.rem(alpha, 2)

    def mask_of(step, which):
        return (1 - which) * 2**step + which * 2 ** (rounds - 1 - step)

    def origin(label, which):
        source = chip
        for step in range(rounds):
            if (label >> step) & 1:
                source = flip(source, mask_of(step, which))
        return source * 2 + which

    if n_beta == n_stops:
        way, far, near = 1 - 2 * core, n_beta // 2, n_beta - 1 - n_beta // 2
    else:
        way, far, near = 1, n_stops - 1, 0
    ahead = lax.rem(beta + way + n_beta, n_beta)
    behind = lax.rem(beta - way + n_beta, n_beta)

    sibling = (alpha + 1 - 2 * core, beta)
    neighbours = [(flip(chip, mask_of(step, core)) * 2 + core, beta) for step in range(rounds)]
    greeted = neighbours + [sibling, (alpha, ahead), (alpha, behind)]
    barrier = pltpu.get_barrier_semaphore()
    for device in greeted:
        pl.semaphore_signal(barrier, inc=1, device_id=device, device_id_type=MESH)
    own = []
    for c in range(chunks):
        own.append(
            pltpu.make_async_copy(c_hbm.at[:, :, pl.ds(starts[c], widths[c])], held[c].at[0], own_sem.at[c])
        )
    own[0].start()
    pl.semaphore_wait(barrier, len(greeted))

    def to_alpha(c, label, target, device):
        source = c_hbm.at[:, :, pl.ds(starts[c], widths[c])] if label == 0 else held[c].at[label]
        return pltpu.make_async_remote_copy(
            src_ref=source,
            dst_ref=held[c].at[target],
            send_sem=send_sem.at[c, target],
            recv_sem=recv_sem.at[c, target],
            device_id=device,
            device_id_type=MESH,
        )

    copies = [{} for _ in range(chunks)]

    def pass_on(c, label):
        for step in range(label.bit_length(), rounds):
            target = label + 2**step
            copies[c][target] = to_alpha(c, label, target, neighbours[step])
            copies[c][target].start()
        target = n_chips + label
        copies[c][target] = to_alpha(c, label, target, sibling)
        copies[c][target].start()

    def slot_of(hop):
        return lax.rem(hop * way + n_beta * n_stops, n_beta)

    hops = [{} for _ in range(chunks)]

    def to_beta(c, kind, hop):
        sign, device, index = (1, ahead, hop - 1) if kind == "far" else (-1, behind, far + hop - 1)
        copy = pltpu.make_async_remote_copy(
            src_ref=moved[c].at[slot_of(sign * (hop - 1))],
            dst_ref=moved[c].at[slot_of(sign * hop)],
            send_sem=zsend_sem.at[c, index],
            recv_sem=zrecv_sem.at[c, index],
            device_id=(alpha, device),
            device_id_type=MESH,
        )
        hops[c][kind, hop] = copy
        copy.start()

    for c in range(min(AHEAD, chunks)):
        if c > 0:
            own[c].start()
        pass_on(c, 0)
    tile_copy = pltpu.make_async_copy(b_hbm, tiles, tile_sem)
    tile_copy.start()

    sources = [origin(label, core) for label in range(n_chips)]
    sources += [origin(label, 1 - core) for label in range(n_chips)]
    picked = []
    for slot, source in enumerate(sources):
        live = counts_ref[source, alpha] == 1
        picked.append(jnp.clip(exc_ref[0, source, alpha] - source * n_blocks, 0, n_blocks - 1))
        target = exc_ref[1, source, alpha] - alpha * n_blocks
        matrix = coupling_ref[exc_ref[2, source, alpha]]
        for block in range(n_blocks):
            keep = jnp.where(live & (target == block), 1.0, 0.0).astype(jnp.float32)
            weights[pl.ds(block * order, order), pl.ds(slot * order, order)] = (
                matrix.astype(jnp.float32) * keep
            ).astype(jnp.bfloat16)

    def product(c):
        @pl.loop(0, out_ref.shape[1] // TILE)
        def _(n):
            columns = pl.ds(pl.multiple_of(n * TILE, TILE), TILE)
            left = jnp.concatenate([moved[c][d] for d in range(n_stops)], axis=1)
            right = jnp.concatenate(
                [tiles[d, pl.ds(starts[c], widths[c]), columns] for d in range(n_stops)], axis=0
            )
            value = jnp.dot(left, right, preferred_element_type=jnp.float32)
            if c == 0:
                out_ref[:, columns] = value
            else:
                out_ref[:, columns] += value

    def relay(c):
        for kind, last in (("far", far), ("near", near)):
            for hop in range(1, last):
                hops[c][kind, hop].wait_recv()
                to_beta(c, kind, hop + 1)

    def finish(c):
        for kind, last in (("far", far), ("near", near)):
            if last > 0:
                hops[c][kind, last].wait_recv()
        if c == 0:
            tile_copy.wait()
        product(c)

    for c in range(chunks):
        for label in range(1, n_chips):
            copies[c][label].wait_recv()
            pass_on(c, label)
            if label == 1 and c + AHEAD < chunks:
                own[c + AHEAD].start()
                pass_on(c + AHEAD, 0)
        own[c].wait()
        for label in range(n_chips):
            copies[c][n_chips + label].wait_recv()
        for slot in range(n_alpha):
            gathered[pl.ds(slot * order, order), pl.ds(0, widths[c])] = held[c][slot, picked[slot]]
        moved[c][0] = jnp.dot(
            weights[...], gathered[:, pl.ds(0, widths[c])], preferred_element_type=jnp.float32
        ).astype(jnp.bfloat16)
        to_beta(c, "far", 1)
        if near > 0:
            to_beta(c, "near", 1)
        if c >= 1:
            relay(c - 1)
        if c >= 2:
            finish(c - 2)
    relay(chunks - 1)
    for c in range(max(chunks - 2, 0), chunks):
        finish(c)
    for c in range(chunks):
        for copy in copies[c].values():
            copy.wait_send()
        for copy in hops[c].values():
            copy.wait_send()


def line_kernel(
    n_alpha, n_beta, rounds, heights,
    exc_hbm, counts_hbm, coupling_hbm, c_hbm, b_hbm, out_ref,
    exc_ref, counts_ref, coupling_ref, weights, tiles, blocks, outer_tiles, partial, remote_sum, held, gathered,
    in_sem, raw_send, raw_recv, sum_send, sum_recv, tile_send, tile_recv, spread_send, spread_recv, spread_last,
    send_sem, recv_sem,
):
    n_chips = n_alpha // 2
    n_blocks, order, columns = c_hbm.shape
    chunks = len(heights)
    offsets = [sum(heights[:c]) for c in range(chunks)]
    alpha, beta = lax.axis_index("alpha"), lax.axis_index("beta")
    chip, core = lax.div(alpha, 2), lax.rem(alpha, 2)
    side = lax.div(beta, 2)
    outer, inner = 3 * side, 1 + side
    across, beyond = 2 - side, 3 - 3 * side
    is_outer = beta == outer

    def mask_of(step, which):
        return (1 - which) * 2**step + which * 2 ** (rounds - 1 - step)

    def origin(label, which):
        source = chip
        for step in range(rounds):
            if (label >> step) & 1:
                source = flip(source, mask_of(step, which))
        return source * 2 + which

    def distance(source):
        return lax.rem(beta - source + n_beta, n_beta)

    sources = [origin(label, core) for label in range(n_chips)]
    sources += [origin(label, 1 - core) for label in range(n_chips)]
    sibling = (alpha + 1 - 2 * core, beta)
    neighbours = [(flip(chip, mask_of(step, core)) * 2 + core, beta) for step in range(rounds)]
    near = (alpha, is_outer.astype(jnp.int32) * inner + (1 - is_outer.astype(jnp.int32)) * outer)
    facing = (alpha, across)

    barrier = pltpu.get_barrier_semaphore()
    for device in neighbours + [sibling, near]:
        pl.semaphore_signal(barrier, inc=1, device_id=device, device_id_type=MESH)

    @pl.when(jnp.logical_not(is_outer))
    def _():
        pl.semaphore_signal(barrier, inc=1, device_id=facing, device_id_type=MESH)

    local = [
        pltpu.make_async_copy(exc_hbm, exc_ref, in_sem.at[0]),
        pltpu.make_async_copy(counts_hbm, counts_ref, in_sem.at[1]),
        pltpu.make_async_copy(coupling_hbm, coupling_ref, in_sem.at[2]),
        pltpu.make_async_copy(c_hbm, blocks.at[beta], in_sem.at[3]),
        pltpu.make_async_copy(b_hbm, tiles, in_sem.at[4]),
    ]
    for copy in local:
        copy.start()
    pl.semaphore_wait(barrier, rounds + 3 - is_outer.astype(jnp.int32))

    def rows_of(c):
        return pl.ds(offsets[c], heights[c])

    def remote(source, target, send, recv, device):
        return pltpu.make_async_remote_copy(
            src_ref=source, dst_ref=target, send_sem=send, recv_sem=recv, device_id=device, device_id_type=MESH
        )

    def raw(c, plane, kind, device):
        source = c_hbm.at[:, rows_of(c)] if kind < 2 else blocks.at[plane, :, rows_of(c)]
        return remote(source, blocks.at[plane, :, rows_of(c)], raw_send.at[kind], raw_recv.at[plane, c], device)

    def sum_copy(c):
        here = remote_sum.at[:, rows_of(c)]
        return remote(here, here, sum_send, sum_recv.at[c], near)

    piece = 2 * b_hbm.shape[1] // n_alpha
    part = piece // PIECES

    def part_of(label, q):
        return pl.ds(pl.multiple_of(sources[label] * piece + q * part, part), part)

    def tile_copy(q):
        row = alpha * piece + q * part
        which = lax.div(row, b_hbm.shape[1])
        tile = (1 - which) * 2 + which * (1 + 2 * side)
        source = b_hbm.at[tile, pl.ds(pl.multiple_of(lax.rem(row, b_hbm.shape[1]), part), part)]
        return remote(source, outer_tiles.at[part_of(0, q)], tile_send, tile_recv.at[q], near)

    def group_of(label):
        return label.bit_count() - 1 if label < n_chips else rounds

    def tile_spread(q, label, target, device):
        here = outer_tiles.at[part_of(label, q)]
        recv = spread_recv.at[q, group_of(target)] if target < n_chips else spread_last
        return remote(here, here, spread_send, recv, device)

    def held_spread(c, label, target, device):
        return remote(
            held[c].at[label], held[c].at[target], send_sem.at[c], recv_sem.at[c, group_of(target)], device
        )

    def spread(make, index, label):
        for step in range(label.bit_length(), rounds):
            make(index, label, label + 2**step, neighbours[step]).start()
        make(index, label, n_chips + label, sibling).start()

    labels_of = [range(1, n_chips - 1), range(n_chips - 1, n_chips), range(n_chips, n_alpha)]

    def tile_relay(q, group):
        count = len(labels_of[group]) * part
        here = outer_tiles.at[pl.ds(0, count)]
        remote(here, here, spread_send, spread_recv.at[q, group], sibling).wait_recv()
        for label in labels_of[group]:
            spread(tile_spread, q, label)

    def held_arrive(c, group):
        labels = labels_of[group]
        here = held[c].at[pl.ds(labels[0], len(labels))]
        remote(here, here, send_sem.at[c], recv_sem.at[c, group], sibling).wait_recv()

    def set_weights():
        for copy in local[:3]:
            copy.wait()
        picked = []
        for slot, source in enumerate(sources):
            live = counts_ref[source, alpha] == 1
            picked.append(jnp.clip(exc_ref[0, source, alpha] - source * n_blocks, 0, n_blocks - 1))
            target = exc_ref[1, source, alpha] - alpha * n_blocks
            matrix = coupling_ref[exc_ref[2, source, alpha]]
            for block in range(n_blocks):
                keep = jnp.where(live & (target == block), 1.0, 0.0).astype(jnp.float32)
                value = (matrix.astype(jnp.float32) * keep).astype(jnp.bfloat16)
                for half in range(order // LANES):
                    weights[half, pl.ds(block * order, order), pl.ds(slot * LANES, LANES)] = value[
                        :, half * LANES : (half + 1) * LANES
                    ]
        return picked

    def product(first, count, planes, tile, store, before=False):
        at_rows = pl.ds(offsets[first], sum(heights[first : first + count]))

        @pl.loop(0, columns // TILE)
        def _(n):
            at = pl.ds(pl.multiple_of(n * TILE, TILE), TILE)
            value = None
            for k, plane in enumerate(planes):
                left = blocks[plane, :, at_rows].reshape(n_blocks * at_rows.size, columns)
                term = jnp.dot(left, tile(k, plane, at), preferred_element_type=jnp.float32)
                value = term if value is None else value + term
            value = value.reshape(n_blocks, at_rows.size, TILE)
            if before:
                value = value + partial[:, at_rows, at]
            store(at_rows, at, value)

    def own_tile(k, plane, at):
        return tiles[distance(plane), :, at]

    def far_tile(k, plane, at):
        return outer_tiles[pl.ds(k * columns, columns), at]

    def store_held(c):
        def store(at_rows, at, value):
            held[c][0, :, :, at] = value.astype(jnp.bfloat16)
        return store

    def store_sum(at_rows, at, value):
        remote_sum[:, at_rows, at] = value.astype(jnp.bfloat16)

    def store_partial(at_rows, at, value):
        partial[:, at_rows, at] = value

    def relay(c, group):
        held_arrive(c, group)
        for label in labels_of[group]:
            spread(held_spread, c, label)

    def finish(c, picked):
        held_arrive(c, rounds)
        half, within = offsets[c] // LANES, offsets[c] % LANES
        for slot in range(n_alpha):
            gathered[half, pl.ds(slot * LANES + within, heights[c])] = held[c][slot, picked[slot]]
        if within + heights[c] == LANES:
            @pl.loop(0, columns // TILE)
            def _(n):
                at = pl.ds(pl.multiple_of(n * TILE, TILE), TILE)
                value = jnp.dot(weights[half], gathered[half, :, at], preferred_element_type=jnp.float32)
                if half == 0:
                    out_ref[:, at] = value
                else:
                    out_ref[:, at] += value

    def advance(group, last, picked):
        while progress[group] <= min(last, chunks - 1):
            if group < rounds:
                relay(progress[group], group)
            else:
                finish(progress[group], picked)
            progress[group] += 1

    def follow(c, lag, picked):
        for group in range(rounds):
            advance(group, c - lag - LAG * group, picked)
        advance(rounds, c - lag - LAG * (rounds - 1) - 1, picked)

    def end(picked):
        advance(rounds, chunks - 1 - 2 * LAG, picked)
        for group in range(rounds - 1):
            advance(group, chunks - 1, picked)
        advance(rounds - 1, chunks - 1 - LAG, picked)
        advance(rounds, chunks - 1 - LAG, picked)
        advance(rounds - 1, chunks - 1, picked)
        advance(rounds, chunks - 1, picked)
        for c in range(chunks):
            here = held[c].at[pl.ds(1, n_alpha - 1)]
            remote(here, here, send_sem.at[c], recv_sem.at[c, 0], sibling).wait_send()

    def sent(ref, sem):
        remote(ref, ref, sem, sum_recv.at[0], near).wait_send()

    progress = [0] * (rounds + 1)

    @pl.when(is_outer)
    def _():
        def own(c):
            raw(c, outer, 0, near).start()

        for q in range(PIECES):
            if q == PIECES // 2:
                own(0)
            tile_copy(q).start()
        for c in range(1, chunks):
            own(c)
        picked = set_weights()
        local[3].wait()
        local[4].wait()

        def prepare(c, count):
            for k in range(c, c + count):
                raw(k, inner, 0, near).wait_recv()
            product(c, count, (outer, inner), own_tile, store_partial)

        def finish_raw(c):
            raw(c, across, 0, near).wait_recv()
            raw(c, beyond, 0, near).wait_recv()
            product(c, 1, (across, beyond), own_tile, store_held(c), before=True)
            spread(held_spread, c, 0)

        prepare(0, 2)
        prepare(2, 2)
        finish_raw(0)
        finish_raw(1)
        follow(1, 1, picked)
        for c in range(RAW, chunks):
            if c == 4:
                prepare(c, 2)
            if c >= SECOND:
                prepare(c, 1)
            sum_copy(c).wait_recv()
            held[c][0] = (
                partial[:, rows_of(c)] + remote_sum[:, rows_of(c)].astype(jnp.float32)
            ).astype(jnp.bfloat16)
            spread(held_spread, c, 0)
            follow(c, 1 if c <= RAW + 1 else LAG, picked)
        end(picked)
        sent(outer_tiles.at[pl.ds(0, piece)], tile_send)
        sent(blocks.at[outer], raw_send.at[0])

    progress = [0] * (rounds + 1)

    @pl.when(jnp.logical_not(is_outer))
    def _():
        def own_near(c):
            raw(c, inner, 0, near).start()

        def own_facing(c):
            raw(c, inner, 1, facing).start()

        for c in range(FIRST):
            if c < 3:
                own_near(c)
            own_facing(c)
        picked = set_weights()
        local[3].wait()
        local[4].wait()

        def prepare(c):
            for k in range(c, c + 2):
                raw(k, across, 1, facing).wait_recv()
            product(c, 2, (inner, across), own_tile, store_partial)

        def pass_on(c):
            if c < chunks:
                raw(c, outer, 0, near).wait_recv()
                raw(c, outer, 2, facing).start()
                if SECOND <= c + 1 < chunks:
                    own_facing(c + 1)

        def tile_own(q):
            tile_copy(q).wait_recv()
            spread(tile_spread, q, 0)

        def finish_held(c):
            product(c, 1, (outer, beyond), own_tile, store_held(c), before=True)
            spread(held_spread, c, 0)

        def send_beyond(c):
            raw(c, beyond, 2, facing).wait_recv()
            raw(c, beyond, 3, near).start()

        def hold(c, lag):
            if c >= FIRST and c % 2 == 0:
                product(c, 2, (inner, across), own_tile, store_partial)
            finish_held(c)
            follow(c, lag, picked)

        def send_across(c):
            raw(c, across, 1, facing).wait_recv()
            raw(c, across, 3, near).start()

        tile_own(0)
        tile_own(1)
        send_across(0)
        send_across(1)
        own_near(3)
        product(0, 2, (inner, across), own_tile, store_partial)
        pass_on(0)
        own_facing(4)
        own_facing(5)
        tile_relay(0, 0)
        tile_own(2)
        tile_relay(1, 0)
        prepare(2)
        tile_own(3)
        tile_relay(0, 1)
        send_beyond(0)
        own_near(4)
        own_near(5)
        tile_relay(2, 0)
        pass_on(1)
        tile_relay(1, 1)
        product(0, 1, (outer, beyond), own_tile, store_held(0), before=True)
        tile_relay(3, 0)
        pass_on(2)
        spread(held_spread, 0, 0)
        tile_relay(2, 1)
        pass_on(3)
        send_beyond(1)
        tile_relay(3, 1)
        hold(1, 1)
        pass_on(4)
        here = outer_tiles.at[pl.ds(0, n_chips * piece)]
        remote(here, here, spread_send, spread_last, sibling).wait_recv()
        for c in range(RAW, chunks):
            if c >= FIRST:
                raw(c, across, 1, facing).wait_recv()
            raw(c, beyond, 2, facing).wait_recv()
            product(c, 1, (across, beyond), far_tile, store_sum)
            sum_copy(c).start()
            if SECOND <= c + 1 < chunks:
                own_near(c + 1)
            pass_on(c + 3)
            if c == RAW:
                hold(c, 1)
            elif c > RAW + 1:
                hold(c - 1, LAG)
        hold(chunks - 1, LAG)
        end(picked)
        sent(outer_tiles.at[pl.ds(0, (n_alpha - 1) * piece)], spread_send)
        sent(remote_sum.at[:, pl.ds(offsets[RAW], order - offsets[RAW])], sum_send)
        for kind in range(3):
            sent(blocks.at[inner], raw_send.at[kind])
        sent(blocks.at[inner, :, pl.ds(0, offsets[2 * RAW])], raw_send.at[3])


def line_call(mesh, coefficients, couplings, exc_list, counts, beta_tiles):
    n_alpha, n_beta = mesh.shape["alpha"], mesh.shape["beta"]
    order = couplings.shape[1]
    rows, columns = coefficients.shape
    n_blocks = rows // order
    heights = [order * share // sum(SHARES) for share in SHARES]
    chunks = len(heights)
    rounds = (n_alpha // 2).bit_length() - 1
    hbm = pl.BlockSpec(memory_space=pl.ANY)
    dma = pltpu.SemaphoreType.DMA
    return pl.pallas_call(
        functools.partial(line_kernel, n_alpha, n_beta, rounds, heights),
        out_shape=pltpu.VMEM((rows, columns), jnp.float32),
        in_specs=[hbm] * 5,
        out_specs=pl.BlockSpec(memory_space=pltpu.VMEM),
        scratch_shapes=[
            pltpu.SMEM((3, n_alpha, n_alpha), jnp.int32),
            pltpu.SMEM((n_alpha, n_alpha), jnp.int32),
            pltpu.VMEM(couplings.shape, jnp.bfloat16),
            pltpu.VMEM((order // LANES, rows, n_alpha * LANES), jnp.bfloat16),
            pltpu.VMEM(beta_tiles.shape, jnp.bfloat16),
            pltpu.VMEM((n_beta, n_blocks, order, columns), jnp.bfloat16),
            pltpu.VMEM((2 * columns, columns), jnp.bfloat16),
            pltpu.VMEM((n_blocks, order, columns), jnp.float32),
            pltpu.VMEM((n_blocks, order, columns), jnp.bfloat16),
            [pltpu.VMEM((n_alpha, n_blocks, height, columns), jnp.bfloat16) for height in heights],
            pltpu.VMEM((order // LANES, n_alpha * LANES, columns), jnp.bfloat16),
            dma((5,)),
            dma((4,)),
            dma((n_beta, chunks)),
            dma(()),
            dma((chunks,)),
            dma(()),
            dma((PIECES,)),
            dma(()),
            dma((PIECES, rounds)),
            dma(()),
            dma((chunks,)),
            dma((chunks, rounds + 1)),
        ],
        compiler_params=pltpu.CompilerParams(
            collective_id=0, has_side_effects=True, vmem_limit_bytes=60 * 2**20
        ),
    )(
        exc_list.transpose(2, 0, 1),
        counts,
        couplings,
        coefficients.reshape(n_blocks, order, columns),
        beta_tiles,
    )


def solution(mesh):
    n_alpha, n_beta = mesh.shape["alpha"], mesh.shape["beta"]
    n_chips = n_alpha // 2
    rounds = n_chips.bit_length() - 1

    def per_device(coefficients, couplings, exc_list, counts, beta_tiles):
        order = couplings.shape[1]
        rows, columns = coefficients.shape
        n_blocks = rows // order
        n_stops = beta_tiles.shape[0]
        if n_alpha == 8 and n_beta == n_stops == 4:
            return line_call(mesh, coefficients, couplings, exc_list, counts, beta_tiles)
        widths, _ = split(columns)
        chunks = len(widths)
        vmem, smem = pl.BlockSpec(memory_space=pltpu.VMEM), pl.BlockSpec(memory_space=pltpu.SMEM)
        hbm = pl.BlockSpec(memory_space=pl.ANY)
        return pl.pallas_call(
            functools.partial(kernel, n_alpha, n_beta, rounds, chunks),
            out_shape=pltpu.VMEM((rows, columns), jnp.float32),
            in_specs=[smem, smem, vmem, hbm, hbm],
            out_specs=vmem,
            scratch_shapes=[
                pltpu.VMEM((rows, n_alpha * order), jnp.bfloat16),
                pltpu.VMEM((n_alpha * order, max(widths)), jnp.bfloat16),
                pltpu.VMEM(beta_tiles.shape, jnp.bfloat16),
                [pltpu.VMEM((n_alpha, n_blocks, order, width), jnp.bfloat16) for width in widths],
                [pltpu.VMEM((n_stops, rows, width), jnp.bfloat16) for width in widths],
                pltpu.SemaphoreType.DMA((chunks, n_alpha)),
                pltpu.SemaphoreType.DMA((chunks, n_alpha)),
                pltpu.SemaphoreType.DMA((chunks,)),
                pltpu.SemaphoreType.DMA((chunks, n_stops - 1)),
                pltpu.SemaphoreType.DMA((chunks, n_stops - 1)),
                pltpu.SemaphoreType.DMA(()),
            ],
            compiler_params=pltpu.CompilerParams(
                collective_id=0, has_side_effects=True, vmem_limit_bytes=48 * 2**20
            ),
        )(
            exc_list.transpose(2, 0, 1),
            counts,
            couplings,
            coefficients.reshape(n_blocks, order, columns),
            beta_tiles,
        )

    placed = (P("alpha", "beta"), P(), P(), P(), P(None, None, "beta"))
    return jax.shard_map(
        per_device, mesh=mesh, in_specs=placed, out_specs=P("alpha", "beta"), check_vma=False
    )
```

```python
import functools

import jax
import jax.numpy as jnp
from jax import lax
from jax.experimental import pallas as pl
from jax.experimental.pallas import tpu as pltpu
from jax.sharding import PartitionSpec as P

MESH = pl.DeviceIdType.MESH
WIDTHS = (1, 2, 2, 2, 1)
TILE = 256
AHEAD = 1
SHARES = (2, 2, 2, 2, 2, 2, 2, 1, 1)
PIECES = 8
LAG = 2
RAW = 2
FIRST = 4
SECOND = 6
LANES = 64


def split(columns):
    unit = columns // sum(WIDTHS)
    widths = [unit * part for part in WIDTHS]
    return widths, [sum(widths[:c]) for c in range(len(widths))]


def flip(position, mask):
    bit = lax.rem(lax.div(position, mask), 2)
    return position + mask * (1 - 2 * bit)


def kernel(
    n_alpha, n_beta, rounds, chunks,
    exc_ref, counts_ref, coupling_ref, c_hbm, b_hbm, out_ref,
    weights, gathered, tiles, held, moved,
    send_sem, recv_sem, own_sem, zsend_sem, zrecv_sem, tile_sem,
):
    n_chips = n_alpha // 2
    n_blocks, order = c_hbm.shape[0], c_hbm.shape[1]
    n_stops = b_hbm.shape[0]
    widths, starts = split(out_ref.shape[1])
    alpha, beta = lax.axis_index("alpha"), lax.axis_index("beta")
    chip, core = lax.div(alpha, 2), lax.rem(alpha, 2)

    def mask_of(step, which):
        return (1 - which) * 2**step + which * 2 ** (rounds - 1 - step)

    def origin(label, which):
        source = chip
        for step in range(rounds):
            if (label >> step) & 1:
                source = flip(source, mask_of(step, which))
        return source * 2 + which

    if n_beta == n_stops:
        way, far, near = 1 - 2 * core, n_beta // 2, n_beta - 1 - n_beta // 2
    else:
        way, far, near = 1, n_stops - 1, 0
    ahead = lax.rem(beta + way + n_beta, n_beta)
    behind = lax.rem(beta - way + n_beta, n_beta)

    sibling = (alpha + 1 - 2 * core, beta)
    neighbours = [(flip(chip, mask_of(step, core)) * 2 + core, beta) for step in range(rounds)]
    greeted = neighbours + [sibling, (alpha, ahead), (alpha, behind)]
    barrier = pltpu.get_barrier_semaphore()
    for device in greeted:
        pl.semaphore_signal(barrier, inc=1, device_id=device, device_id_type=MESH)
    own = []
    for c in range(chunks):
        own.append(
            pltpu.make_async_copy(c_hbm.at[:, :, pl.ds(starts[c], widths[c])], held[c].at[0], own_sem.at[c])
        )
    own[0].start()
    pl.semaphore_wait(barrier, len(greeted))

    def to_alpha(c, label, target, device):
        source = c_hbm.at[:, :, pl.ds(starts[c], widths[c])] if label == 0 else held[c].at[label]
        return pltpu.make_async_remote_copy(
            src_ref=source,
            dst_ref=held[c].at[target],
            send_sem=send_sem.at[c, target],
            recv_sem=recv_sem.at[c, target],
            device_id=device,
            device_id_type=MESH,
        )

    copies = [{} for _ in range(chunks)]

    def pass_on(c, label):
        for step in range(label.bit_length(), rounds):
            target = label + 2**step
            copies[c][target] = to_alpha(c, label, target, neighbours[step])
            copies[c][target].start()
        target = n_chips + label
        copies[c][target] = to_alpha(c, label, target, sibling)
        copies[c][target].start()

    def slot_of(hop):
        return lax.rem(hop * way + n_beta * n_stops, n_beta)

    hops = [{} for _ in range(chunks)]

    def to_beta(c, kind, hop):
        sign, device, index = (1, ahead, hop - 1) if kind == "far" else (-1, behind, far + hop - 1)
        copy = pltpu.make_async_remote_copy(
            src_ref=moved[c].at[slot_of(sign * (hop - 1))],
            dst_ref=moved[c].at[slot_of(sign * hop)],
            send_sem=zsend_sem.at[c, index],
            recv_sem=zrecv_sem.at[c, index],
            device_id=(alpha, device),
            device_id_type=MESH,
        )
        hops[c][kind, hop] = copy
        copy.start()

    for c in range(min(AHEAD, chunks)):
        if c > 0:
            own[c].start()
        pass_on(c, 0)
    tile_copy = pltpu.make_async_copy(b_hbm, tiles, tile_sem)
    tile_copy.start()

    sources = [origin(label, core) for label in range(n_chips)]
    sources += [origin(label, 1 - core) for label in range(n_chips)]
    picked = []
    for slot, source in enumerate(sources):
        live = counts_ref[source, alpha] == 1
        picked.append(jnp.clip(exc_ref[0, source, alpha] - source * n_blocks, 0, n_blocks - 1))
        target = exc_ref[1, source, alpha] - alpha * n_blocks
        matrix = coupling_ref[exc_ref[2, source, alpha]]
        for block in range(n_blocks):
            keep = jnp.where(live & (target == block), 1.0, 0.0).astype(jnp.float32)
            weights[pl.ds(block * order, order), pl.ds(slot * order, order)] = (
                matrix.astype(jnp.float32) * keep
            ).astype(jnp.bfloat16)

    def product(c):
        @pl.loop(0, out_ref.shape[1] // TILE)
        def _(n):
            columns = pl.ds(pl.multiple_of(n * TILE, TILE), TILE)
            left = jnp.concatenate([moved[c][d] for d in range(n_stops)], axis=1)
            right = jnp.concatenate(
                [tiles[d, pl.ds(starts[c], widths[c]), columns] for d in range(n_stops)], axis=0
            )
            value = jnp.dot(left, right, preferred_element_type=jnp.float32)
            if c == 0:
                out_ref[:, columns] = value
            else:
                out_ref[:, columns] += value

    def relay(c):
        for kind, last in (("far", far), ("near", near)):
            for hop in range(1, last):
                hops[c][kind, hop].wait_recv()
                to_beta(c, kind, hop + 1)

    def finish(c):
        for kind, last in (("far", far), ("near", near)):
            if last > 0:
                hops[c][kind, last].wait_recv()
        if c == 0:
            tile_copy.wait()
        product(c)

    for c in range(chunks):
        for label in range(1, n_chips):
            copies[c][label].wait_recv()
            pass_on(c, label)
            if label == 1 and c + AHEAD < chunks:
                own[c + AHEAD].start()
                pass_on(c + AHEAD, 0)
        own[c].wait()
        for label in range(n_chips):
            copies[c][n_chips + label].wait_recv()
        for slot in range(n_alpha):
            gathered[pl.ds(slot * order, order), pl.ds(0, widths[c])] = held[c][slot, picked[slot]]
        moved[c][0] = jnp.dot(
            weights[...], gathered[:, pl.ds(0, widths[c])], preferred_element_type=jnp.float32
        ).astype(jnp.bfloat16)
        to_beta(c, "far", 1)
        if near > 0:
            to_beta(c, "near", 1)
        if c >= 1:
            relay(c - 1)
        if c >= 2:
            finish(c - 2)
    relay(chunks - 1)
    for c in range(max(chunks - 2, 0), chunks):
        finish(c)
    for c in range(chunks):
        for copy in copies[c].values():
            copy.wait_send()
        for copy in hops[c].values():
            copy.wait_send()


def line_kernel(
    n_alpha, n_beta, rounds, heights,
    exc_hbm, counts_hbm, coupling_hbm, c_hbm, b_hbm, out_ref, last_weights, last_gathered,
    exc_ref, counts_ref, coupling_ref, weights, tiles, blocks, outer_tiles, partial, remote_sum, held, gathered,
    in_sem, raw_send, raw_recv, sum_send, sum_recv, tile_send, tile_recv, spread_send, spread_recv, spread_last,
    send_sem, recv_sem,
):
    n_chips = n_alpha // 2
    n_blocks, order, columns = c_hbm.shape
    chunks = len(heights)
    offsets = [sum(heights[:c]) for c in range(chunks)]
    alpha, beta = lax.axis_index("alpha"), lax.axis_index("beta")
    chip, core = lax.div(alpha, 2), lax.rem(alpha, 2)
    side = lax.div(beta, 2)
    outer, inner = 3 * side, 1 + side
    across, beyond = 2 - side, 3 - 3 * side
    is_outer = beta == outer

    def mask_of(step, which):
        return (1 - which) * 2**step + which * 2 ** (rounds - 1 - step)

    def origin(label, which):
        source = chip
        for step in range(rounds):
            if (label >> step) & 1:
                source = flip(source, mask_of(step, which))
        return source * 2 + which

    def distance(source):
        return lax.rem(beta - source + n_beta, n_beta)

    sources = [origin(label, core) for label in range(n_chips)]
    sources += [origin(label, 1 - core) for label in range(n_chips)]
    sibling = (alpha + 1 - 2 * core, beta)
    neighbours = [(flip(chip, mask_of(step, core)) * 2 + core, beta) for step in range(rounds)]
    near = (alpha, is_outer.astype(jnp.int32) * inner + (1 - is_outer.astype(jnp.int32)) * outer)
    facing = (alpha, across)

    barrier = pltpu.get_barrier_semaphore()
    for device in neighbours + [sibling, near]:
        pl.semaphore_signal(barrier, inc=1, device_id=device, device_id_type=MESH)

    @pl.when(jnp.logical_not(is_outer))
    def _():
        pl.semaphore_signal(barrier, inc=1, device_id=facing, device_id_type=MESH)

    local = [
        pltpu.make_async_copy(exc_hbm, exc_ref, in_sem.at[0]),
        pltpu.make_async_copy(counts_hbm, counts_ref, in_sem.at[1]),
        pltpu.make_async_copy(coupling_hbm, coupling_ref, in_sem.at[2]),
        pltpu.make_async_copy(c_hbm, blocks.at[beta], in_sem.at[3]),
        pltpu.make_async_copy(b_hbm, tiles, in_sem.at[4]),
    ]
    for copy in local:
        copy.start()
    pl.semaphore_wait(barrier, rounds + 3 - is_outer.astype(jnp.int32))

    def rows_of(c):
        return pl.ds(offsets[c], heights[c])

    def remote(source, target, send, recv, device):
        return pltpu.make_async_remote_copy(
            src_ref=source, dst_ref=target, send_sem=send, recv_sem=recv, device_id=device, device_id_type=MESH
        )

    def raw(c, plane, kind, device):
        source = c_hbm.at[:, rows_of(c)] if kind < 2 else blocks.at[plane, :, rows_of(c)]
        return remote(source, blocks.at[plane, :, rows_of(c)], raw_send.at[kind], raw_recv.at[plane, c], device)

    def sum_copy(c, first=0, width=columns):
        here = remote_sum.at[:, rows_of(c), pl.ds(first, width)]
        return remote(here, here, sum_send, sum_recv.at[c], near)

    piece = 2 * b_hbm.shape[1] // n_alpha
    part = piece // PIECES

    def part_of(label, q):
        return pl.ds(pl.multiple_of(sources[label] * piece + q * part, part), part)

    def tile_copy(q):
        row = alpha * piece + q * part
        which = lax.div(row, b_hbm.shape[1])
        tile = (1 - which) * 2 + which * (1 + 2 * side)
        source = b_hbm.at[tile, pl.ds(pl.multiple_of(lax.rem(row, b_hbm.shape[1]), part), part)]
        return remote(source, outer_tiles.at[part_of(0, q)], tile_send, tile_recv.at[q], near)

    def group_of(label):
        return label.bit_count() - 1 if label < n_chips else rounds

    def tile_spread(q, label, target, device):
        here = outer_tiles.at[part_of(label, q)]
        recv = spread_recv.at[q, group_of(target)] if target < n_chips else spread_last
        return remote(here, here, spread_send, recv, device)

    def held_spread(c, label, target, device):
        return remote(
            held[c].at[label], held[c].at[target], send_sem.at[c], recv_sem.at[c, group_of(target)], device
        )

    def spread(make, index, label):
        for step in range(label.bit_length(), rounds):
            make(index, label, label + 2**step, neighbours[step]).start()
        make(index, label, n_chips + label, sibling).start()

    labels_of = [range(1, n_chips - 1), range(n_chips - 1, n_chips), range(n_chips, n_alpha)]

    def tile_relay(q, group):
        count = len(labels_of[group]) * part
        here = outer_tiles.at[pl.ds(0, count)]
        remote(here, here, spread_send, spread_recv.at[q, group], sibling).wait_recv()
        for label in labels_of[group]:
            spread(tile_spread, q, label)

    def held_arrive(c, group):
        labels = labels_of[group]
        here = held[c].at[pl.ds(labels[0], len(labels))]
        remote(here, here, send_sem.at[c], recv_sem.at[c, group], sibling).wait_recv()

    def set_weights():
        for copy in local[:3]:
            copy.wait()
        picked = []
        for slot, source in enumerate(sources):
            live = counts_ref[source, alpha] == 1
            picked.append(jnp.clip(exc_ref[0, source, alpha] - source * n_blocks, 0, n_blocks - 1))
            target = exc_ref[1, source, alpha] - alpha * n_blocks
            matrix = coupling_ref[exc_ref[2, source, alpha]]
            for block in range(n_blocks):
                keep = jnp.where(live & (target == block), 1.0, 0.0).astype(jnp.float32)
                value = (matrix.astype(jnp.float32) * keep).astype(jnp.bfloat16)
                at = (pl.ds(block * order, order), pl.ds(slot * LANES, LANES))
                for half in range(order // LANES - 1):
                    weights[(half, *at)] = value[:, half * LANES : (half + 1) * LANES]
                last_weights[at] = value[:, order - LANES :]
        return picked

    def product(first, count, planes, tile, store, before=False, start=0, stop=columns):
        at_rows = pl.ds(offsets[first], sum(heights[first : first + count]))

        @pl.loop(start // TILE, stop // TILE)
        def _(n):
            at = pl.ds(pl.multiple_of(n * TILE, TILE), TILE)
            value = None
            for k, plane in enumerate(planes):
                left = blocks[plane, :, at_rows].reshape(n_blocks * at_rows.size, columns)
                term = jnp.dot(left, tile(k, plane, at), preferred_element_type=jnp.float32)
                value = term if value is None else value + term
            value = value.reshape(n_blocks, at_rows.size, TILE)
            if before:
                value = value + partial[:, at_rows, at]
            store(at_rows, at, value)

    def own_tile(k, plane, at):
        return tiles[distance(plane), :, at]

    def far_tile(k, plane, at):
        return outer_tiles[pl.ds(k * columns, columns), at]

    def store_held(c):
        def store(at_rows, at, value):
            held[c][0, :, :, at] = value.astype(jnp.bfloat16)
        return store

    def store_sum(at_rows, at, value):
        remote_sum[:, at_rows, at] = value.astype(jnp.bfloat16)

    def store_partial(at_rows, at, value):
        partial[:, at_rows, at] = value

    def relay(c, group):
        held_arrive(c, group)
        for label in labels_of[group]:
            spread(held_spread, c, label)

    def finish(c, picked):
        held_arrive(c, rounds)
        half, within = offsets[c] // LANES, offsets[c] % LANES
        final = half == order // LANES - 1
        panel = last_gathered if final else gathered.at[half]
        for slot in range(n_alpha):
            panel[pl.ds(slot * LANES + within, heights[c])] = held[c][slot, picked[slot]]
        if within + heights[c] == LANES and not final:
            @pl.loop(0, columns // TILE)
            def _(n):
                at = pl.ds(pl.multiple_of(n * TILE, TILE), TILE)
                value = jnp.dot(weights[half], gathered[half, :, at], preferred_element_type=jnp.float32)
                if half == 0:
                    out_ref[:, at] = value
                else:
                    out_ref[:, at] += value

    def advance(group, last, picked):
        while progress[group] <= min(last, chunks - 1):
            if group < rounds:
                relay(progress[group], group)
            else:
                finish(progress[group], picked)
            progress[group] += 1

    def follow(c, lag, picked):
        for group in range(rounds):
            advance(group, c - lag - LAG * group, picked)
        advance(rounds, c - lag - LAG * (rounds - 1) - 1, picked)

    def end(picked):
        advance(rounds, chunks - 1 - 2 * LAG, picked)
        for group in range(rounds - 1):
            advance(group, chunks - 1, picked)
        advance(rounds - 1, chunks - 2 - LAG, picked)
        advance(rounds, chunks - 2 - LAG, picked)
        advance(rounds - 1, chunks - 1, picked)
        advance(rounds, chunks - 1, picked)
        for c in range(chunks):
            here = held[c].at[pl.ds(1, n_alpha - 1)]
            remote(here, here, send_sem.at[c], recv_sem.at[c, 0], sibling).wait_send()

    def sent(ref, sem):
        remote(ref, ref, sem, sum_recv.at[0], near).wait_send()

    progress = [0] * (rounds + 1)

    @pl.when(is_outer)
    def _():
        def own(c):
            raw(c, outer, 0, near).start()

        for q in range(PIECES):
            if q == PIECES // 2:
                own(0)
            tile_copy(q).start()
        for c in range(1, chunks):
            own(c)
        picked = set_weights()
        local[3].wait()
        local[4].wait()

        def prepare(c, count):
            for k in range(c, c + count):
                raw(k, inner, 0, near).wait_recv()
            product(c, count, (outer, inner), own_tile, store_partial)

        def finish_raw(c):
            raw(c, across, 0, near).wait_recv()
            raw(c, beyond, 0, near).wait_recv()
            product(c, 1, (across, beyond), own_tile, store_held(c), before=True)
            spread(held_spread, c, 0)

        prepare(0, 2)
        prepare(2, 2)
        finish_raw(0)
        finish_raw(1)
        follow(1, 1, picked)
        for c in range(RAW, chunks):
            if c == 4:
                prepare(c, 2)
            if c >= SECOND:
                prepare(c, 1)
            sum_copy(c).wait_recv()
            held[c][0] = (
                partial[:, rows_of(c)] + remote_sum[:, rows_of(c)].astype(jnp.float32)
            ).astype(jnp.bfloat16)
            spread(held_spread, c, 0)
            follow(c, 1 if c <= RAW + 1 else LAG, picked)
        end(picked)
        sent(outer_tiles.at[pl.ds(0, piece)], tile_send)
        sent(blocks.at[outer], raw_send.at[0])

    progress = [0] * (rounds + 1)

    @pl.when(jnp.logical_not(is_outer))
    def _():
        def own_near(c):
            raw(c, inner, 0, near).start()

        def own_facing(c):
            raw(c, inner, 1, facing).start()

        for c in range(FIRST):
            if c < 3:
                own_near(c)
            own_facing(c)
        picked = set_weights()
        local[3].wait()
        local[4].wait()

        def prepare(c):
            for k in range(c, c + 2):
                raw(k, across, 1, facing).wait_recv()
            product(c, 2, (inner, across), own_tile, store_partial)

        def pass_on(c):
            if c < chunks:
                raw(c, outer, 0, near).wait_recv()
                raw(c, outer, 2, facing).start()
                if SECOND <= c + 1 < chunks:
                    own_facing(c + 1)

        def tile_own(pair):
            for q in (2 * pair, 2 * pair + 1):
                tile_copy(q).wait_recv()
                spread(tile_spread, q, 0)

        def tile_pass(pair, group):
            for q in (2 * pair, 2 * pair + 1):
                tile_relay(q, group)

        def finish_held(c):
            product(c, 1, (outer, beyond), own_tile, store_held(c), before=True)
            spread(held_spread, c, 0)

        def send_beyond(c):
            raw(c, beyond, 2, facing).wait_recv()
            raw(c, beyond, 3, near).start()

        def hold(c, lag):
            if c >= FIRST and c % 2 == 0:
                product(c, min(2, chunks - c), (inner, across), own_tile, store_partial)
            finish_held(c)
            follow(c, lag, picked)

        def send_across(c):
            raw(c, across, 1, facing).wait_recv()
            raw(c, across, 3, near).start()

        tile_own(0)
        tile_own(1)
        send_across(0)
        send_across(1)
        own_near(3)
        product(0, 2, (inner, across), own_tile, store_partial)
        pass_on(0)
        own_facing(4)
        own_facing(5)
        tile_pass(0, 0)
        tile_own(2)
        tile_pass(1, 0)
        prepare(2)
        tile_own(3)
        tile_pass(0, 1)
        send_beyond(0)
        own_near(4)
        own_near(5)
        tile_pass(2, 0)
        pass_on(1)
        tile_pass(1, 1)
        product(0, 1, (outer, beyond), own_tile, store_held(0), before=True)
        tile_pass(3, 0)
        pass_on(2)
        spread(held_spread, 0, 0)
        tile_pass(2, 1)
        pass_on(3)
        send_beyond(1)
        tile_pass(3, 1)
        hold(1, 1)
        pass_on(4)
        here = outer_tiles.at[pl.ds(0, n_chips * piece)]
        remote(here, here, spread_send, spread_last, sibling).wait_recv()
        for c in range(RAW, chunks):
            if c >= FIRST:
                raw(c, across, 1, facing).wait_recv()
            raw(c, beyond, 2, facing).wait_recv()
            for first in range(0, columns, columns // 2):
                product(c, 1, (across, beyond), far_tile, store_sum, start=first, stop=first + columns // 2)
                sum_copy(c, first, columns // 2).start()
            if SECOND <= c + 1 < chunks:
                own_near(c + 1)
            pass_on(c + 3)
            if c == RAW:
                hold(c, 1)
            elif c > RAW + 1:
                hold(c - 1, LAG)
        hold(chunks - 1, LAG)
        end(picked)
        sent(outer_tiles.at[pl.ds(0, (n_alpha - 1) * piece)], spread_send)
        sent(remote_sum.at[:, pl.ds(offsets[RAW], order - offsets[RAW])], sum_send)
        for kind in range(3):
            sent(blocks.at[inner], raw_send.at[kind])
        sent(blocks.at[inner, :, pl.ds(0, offsets[2 * RAW])], raw_send.at[3])


def line_call(mesh, coefficients, couplings, exc_list, counts, beta_tiles):
    n_alpha, n_beta = mesh.shape["alpha"], mesh.shape["beta"]
    order = couplings.shape[1]
    rows, columns = coefficients.shape
    n_blocks = rows // order
    heights = [order * share // sum(SHARES) for share in SHARES]
    chunks = len(heights)
    rounds = (n_alpha // 2).bit_length() - 1
    hbm = pl.BlockSpec(memory_space=pl.ANY)
    dma = pltpu.SemaphoreType.DMA
    total, last_weights, last_gathered = pl.pallas_call(
        functools.partial(line_kernel, n_alpha, n_beta, rounds, heights),
        out_shape=[
            pltpu.VMEM((rows, columns), jnp.float32),
            pltpu.VMEM((rows, n_alpha * LANES), jnp.bfloat16),
            pltpu.VMEM((n_alpha * LANES, columns), jnp.bfloat16),
        ],
        in_specs=[hbm] * 5,
        out_specs=[pl.BlockSpec(memory_space=pltpu.VMEM)] * 3,
        scratch_shapes=[
            pltpu.SMEM((3, n_alpha, n_alpha), jnp.int32),
            pltpu.SMEM((n_alpha, n_alpha), jnp.int32),
            pltpu.VMEM(couplings.shape, jnp.bfloat16),
            pltpu.VMEM((order // LANES - 1, rows, n_alpha * LANES), jnp.bfloat16),
            pltpu.VMEM(beta_tiles.shape, jnp.bfloat16),
            pltpu.VMEM((n_beta, n_blocks, order, columns), jnp.bfloat16),
            pltpu.VMEM((2 * columns, columns), jnp.bfloat16),
            pltpu.VMEM((n_blocks, order, columns), jnp.float32),
            pltpu.VMEM((n_blocks, order, columns), jnp.bfloat16),
            [pltpu.VMEM((n_alpha, n_blocks, height, columns), jnp.bfloat16) for height in heights],
            pltpu.VMEM((order // LANES - 1, n_alpha * LANES, columns), jnp.bfloat16),
            dma((5,)),
            dma((4,)),
            dma((n_beta, chunks)),
            dma(()),
            dma((chunks,)),
            dma(()),
            dma((PIECES,)),
            dma(()),
            dma((PIECES, rounds)),
            dma(()),
            dma((chunks,)),
            dma((chunks, rounds + 1)),
        ],
        compiler_params=pltpu.CompilerParams(
            collective_id=0, has_side_effects=True, vmem_limit_bytes=60 * 2**20
        ),
    )(
        exc_list.transpose(2, 0, 1),
        counts,
        couplings,
        coefficients.reshape(n_blocks, order, columns),
        beta_tiles,
    )
    return total + jnp.dot(last_weights, last_gathered, preferred_element_type=jnp.float32)


def solution(mesh):
    n_alpha, n_beta = mesh.shape["alpha"], mesh.shape["beta"]
    n_chips = n_alpha // 2
    rounds = n_chips.bit_length() - 1

    def per_device(coefficients, couplings, exc_list, counts, beta_tiles):
        order = couplings.shape[1]
        rows, columns = coefficients.shape
        n_blocks = rows // order
        n_stops = beta_tiles.shape[0]
        if n_alpha == 8 and n_beta == n_stops == 4:
            return line_call(mesh, coefficients, couplings, exc_list, counts, beta_tiles)
        widths, _ = split(columns)
        chunks = len(widths)
        vmem, smem = pl.BlockSpec(memory_space=pltpu.VMEM), pl.BlockSpec(memory_space=pltpu.SMEM)
        hbm = pl.BlockSpec(memory_space=pl.ANY)
        return pl.pallas_call(
            functools.partial(kernel, n_alpha, n_beta, rounds, chunks),
            out_shape=pltpu.VMEM((rows, columns), jnp.float32),
            in_specs=[smem, smem, vmem, hbm, hbm],
            out_specs=vmem,
            scratch_shapes=[
                pltpu.VMEM((rows, n_alpha * order), jnp.bfloat16),
                pltpu.VMEM((n_alpha * order, max(widths)), jnp.bfloat16),
                pltpu.VMEM(beta_tiles.shape, jnp.bfloat16),
                [pltpu.VMEM((n_alpha, n_blocks, order, width), jnp.bfloat16) for width in widths],
                [pltpu.VMEM((n_stops, rows, width), jnp.bfloat16) for width in widths],
                pltpu.SemaphoreType.DMA((chunks, n_alpha)),
                pltpu.SemaphoreType.DMA((chunks, n_alpha)),
                pltpu.SemaphoreType.DMA((chunks,)),
                pltpu.SemaphoreType.DMA((chunks, n_stops - 1)),
                pltpu.SemaphoreType.DMA((chunks, n_stops - 1)),
                pltpu.SemaphoreType.DMA(()),
            ],
            compiler_params=pltpu.CompilerParams(
                collective_id=0, has_side_effects=True, vmem_limit_bytes=48 * 2**20
            ),
        )(
            exc_list.transpose(2, 0, 1),
            counts,
            couplings,
            coefficients.reshape(n_blocks, order, columns),
            beta_tiles,
        )

    placed = (P("alpha", "beta"), P(), P(), P(), P(None, None, "beta"))
    return jax.shard_map(
        per_device, mesh=mesh, in_specs=placed, out_specs=P("alpha", "beta"), check_vma=False
    )
```

```python
import functools

import jax
import jax.numpy as jnp
from jax import lax
from jax.experimental import pallas as pl
from jax.experimental.pallas import tpu as pltpu
from jax.sharding import PartitionSpec as P

MESH = pl.DeviceIdType.MESH
WIDTHS = (1, 2, 2, 2, 1)
TILE = 256
AHEAD = 1
SHARES = (2, 2, 2, 2, 2, 2, 2, 1, 1)
PIECES = 8
LAG = 2
RAW = 2
FIRST = 4
SECOND = 6
LANES = 64


def split(columns):
    unit = columns // sum(WIDTHS)
    widths = [unit * part for part in WIDTHS]
    return widths, [sum(widths[:c]) for c in range(len(widths))]


def flip(position, mask):
    bit = lax.rem(lax.div(position, mask), 2)
    return position + mask * (1 - 2 * bit)


def kernel(
    n_alpha, n_beta, rounds, chunks,
    exc_ref, counts_ref, coupling_ref, c_hbm, b_hbm, out_ref,
    weights, gathered, tiles, held, moved,
    send_sem, recv_sem, own_sem, zsend_sem, zrecv_sem, tile_sem,
):
    n_chips = n_alpha // 2
    n_blocks, order = c_hbm.shape[0], c_hbm.shape[1]
    n_stops = b_hbm.shape[0]
    widths, starts = split(out_ref.shape[1])
    alpha, beta = lax.axis_index("alpha"), lax.axis_index("beta")
    chip, core = lax.div(alpha, 2), lax.rem(alpha, 2)

    def mask_of(step, which):
        return (1 - which) * 2**step + which * 2 ** (rounds - 1 - step)

    def origin(label, which):
        source = chip
        for step in range(rounds):
            if (label >> step) & 1:
                source = flip(source, mask_of(step, which))
        return source * 2 + which

    if n_beta == n_stops:
        way, far, near = 1 - 2 * core, n_beta // 2, n_beta - 1 - n_beta // 2
    else:
        way, far, near = 1, n_stops - 1, 0
    ahead = lax.rem(beta + way + n_beta, n_beta)
    behind = lax.rem(beta - way + n_beta, n_beta)

    sibling = (alpha + 1 - 2 * core, beta)
    neighbours = [(flip(chip, mask_of(step, core)) * 2 + core, beta) for step in range(rounds)]
    greeted = neighbours + [sibling, (alpha, ahead), (alpha, behind)]
    barrier = pltpu.get_barrier_semaphore()
    for device in greeted:
        pl.semaphore_signal(barrier, inc=1, device_id=device, device_id_type=MESH)
    own = []
    for c in range(chunks):
        own.append(
            pltpu.make_async_copy(c_hbm.at[:, :, pl.ds(starts[c], widths[c])], held[c].at[0], own_sem.at[c])
        )
    own[0].start()
    pl.semaphore_wait(barrier, len(greeted))

    def to_alpha(c, label, target, device):
        source = c_hbm.at[:, :, pl.ds(starts[c], widths[c])] if label == 0 else held[c].at[label]
        return pltpu.make_async_remote_copy(
            src_ref=source,
            dst_ref=held[c].at[target],
            send_sem=send_sem.at[c, target],
            recv_sem=recv_sem.at[c, target],
            device_id=device,
            device_id_type=MESH,
        )

    copies = [{} for _ in range(chunks)]

    def pass_on(c, label):
        for step in range(label.bit_length(), rounds):
            target = label + 2**step
            copies[c][target] = to_alpha(c, label, target, neighbours[step])
            copies[c][target].start()
        target = n_chips + label
        copies[c][target] = to_alpha(c, label, target, sibling)
        copies[c][target].start()

    def slot_of(hop):
        return lax.rem(hop * way + n_beta * n_stops, n_beta)

    hops = [{} for _ in range(chunks)]

    def to_beta(c, kind, hop):
        sign, device, index = (1, ahead, hop - 1) if kind == "far" else (-1, behind, far + hop - 1)
        copy = pltpu.make_async_remote_copy(
            src_ref=moved[c].at[slot_of(sign * (hop - 1))],
            dst_ref=moved[c].at[slot_of(sign * hop)],
            send_sem=zsend_sem.at[c, index],
            recv_sem=zrecv_sem.at[c, index],
            device_id=(alpha, device),
            device_id_type=MESH,
        )
        hops[c][kind, hop] = copy
        copy.start()

    for c in range(min(AHEAD, chunks)):
        if c > 0:
            own[c].start()
        pass_on(c, 0)
    tile_copy = pltpu.make_async_copy(b_hbm, tiles, tile_sem)
    tile_copy.start()

    sources = [origin(label, core) for label in range(n_chips)]
    sources += [origin(label, 1 - core) for label in range(n_chips)]
    picked = []
    for slot, source in enumerate(sources):
        live = counts_ref[source, alpha] == 1
        picked.append(jnp.clip(exc_ref[0, source, alpha] - source * n_blocks, 0, n_blocks - 1))
        target = exc_ref[1, source, alpha] - alpha * n_blocks
        matrix = coupling_ref[exc_ref[2, source, alpha]]
        for block in range(n_blocks):
            keep = jnp.where(live & (target == block), 1.0, 0.0).astype(jnp.float32)
            weights[pl.ds(block * order, order), pl.ds(slot * order, order)] = (
                matrix.astype(jnp.float32) * keep
            ).astype(jnp.bfloat16)

    def product(c):
        @pl.loop(0, out_ref.shape[1] // TILE)
        def _(n):
            columns = pl.ds(pl.multiple_of(n * TILE, TILE), TILE)
            left = jnp.concatenate([moved[c][d] for d in range(n_stops)], axis=1)
            right = jnp.concatenate(
                [tiles[d, pl.ds(starts[c], widths[c]), columns] for d in range(n_stops)], axis=0
            )
            value = jnp.dot(left, right, preferred_element_type=jnp.float32)
            if c == 0:
                out_ref[:, columns] = value
            else:
                out_ref[:, columns] += value

    def relay(c):
        for kind, last in (("far", far), ("near", near)):
            for hop in range(1, last):
                hops[c][kind, hop].wait_recv()
                to_beta(c, kind, hop + 1)

    def finish(c):
        for kind, last in (("far", far), ("near", near)):
            if last > 0:
                hops[c][kind, last].wait_recv()
        if c == 0:
            tile_copy.wait()
        product(c)

    for c in range(chunks):
        for label in range(1, n_chips):
            copies[c][label].wait_recv()
            pass_on(c, label)
            if label == 1 and c + AHEAD < chunks:
                own[c + AHEAD].start()
                pass_on(c + AHEAD, 0)
        own[c].wait()
        for label in range(n_chips):
            copies[c][n_chips + label].wait_recv()
        for slot in range(n_alpha):
            gathered[pl.ds(slot * order, order), pl.ds(0, widths[c])] = held[c][slot, picked[slot]]
        moved[c][0] = jnp.dot(
            weights[...], gathered[:, pl.ds(0, widths[c])], preferred_element_type=jnp.float32
        ).astype(jnp.bfloat16)
        to_beta(c, "far", 1)
        if near > 0:
            to_beta(c, "near", 1)
        if c >= 1:
            relay(c - 1)
        if c >= 2:
            finish(c - 2)
    relay(chunks - 1)
    for c in range(max(chunks - 2, 0), chunks):
        finish(c)
    for c in range(chunks):
        for copy in copies[c].values():
            copy.wait_send()
        for copy in hops[c].values():
            copy.wait_send()


def line_kernel(
    n_alpha, n_beta, rounds, heights,
    exc_hbm, counts_hbm, coupling_hbm, c_hbm, b_hbm, out_ref, last_weights, last_gathered,
    exc_ref, counts_ref, coupling_ref, weights, tiles, blocks, outer_tiles, partial, remote_sum, held, gathered,
    in_sem, raw_send, raw_recv, sum_send, sum_recv, tile_send, tile_recv, spread_send, spread_recv, spread_last,
    send_sem, recv_sem,
):
    n_chips = n_alpha // 2
    n_blocks, order, columns = c_hbm.shape
    chunks = len(heights)
    offsets = [sum(heights[:c]) for c in range(chunks)]
    alpha, beta = lax.axis_index("alpha"), lax.axis_index("beta")
    chip, core = lax.div(alpha, 2), lax.rem(alpha, 2)
    side = lax.div(beta, 2)
    outer, inner = 3 * side, 1 + side
    across, beyond = 2 - side, 3 - 3 * side
    is_outer = beta == outer

    def mask_of(step, which):
        return (1 - which) * 2**step + which * 2 ** (rounds - 1 - step)

    def origin(label, which):
        source = chip
        for step in range(rounds):
            if (label >> step) & 1:
                source = flip(source, mask_of(step, which))
        return source * 2 + which

    def distance(source):
        return lax.rem(beta - source + n_beta, n_beta)

    sources = [origin(label, core) for label in range(n_chips)]
    sources += [origin(label, 1 - core) for label in range(n_chips)]
    sibling = (alpha + 1 - 2 * core, beta)
    neighbours = [(flip(chip, mask_of(step, core)) * 2 + core, beta) for step in range(rounds)]
    near = (alpha, is_outer.astype(jnp.int32) * inner + (1 - is_outer.astype(jnp.int32)) * outer)
    facing = (alpha, across)

    barrier = pltpu.get_barrier_semaphore()
    for device in neighbours + [sibling, near]:
        pl.semaphore_signal(barrier, inc=1, device_id=device, device_id_type=MESH)

    @pl.when(jnp.logical_not(is_outer))
    def _():
        pl.semaphore_signal(barrier, inc=1, device_id=facing, device_id_type=MESH)

    local = [
        pltpu.make_async_copy(exc_hbm, exc_ref, in_sem.at[0]),
        pltpu.make_async_copy(counts_hbm, counts_ref, in_sem.at[1]),
        pltpu.make_async_copy(coupling_hbm, coupling_ref, in_sem.at[2]),
        pltpu.make_async_copy(c_hbm, blocks.at[beta], in_sem.at[3]),
        pltpu.make_async_copy(b_hbm, tiles, in_sem.at[4]),
    ]
    for copy in local:
        copy.start()
    pl.semaphore_wait(barrier, rounds + 3 - is_outer.astype(jnp.int32))

    def rows_of(c):
        return pl.ds(offsets[c], heights[c])

    def remote(source, target, send, recv, device):
        return pltpu.make_async_remote_copy(
            src_ref=source, dst_ref=target, send_sem=send, recv_sem=recv, device_id=device, device_id_type=MESH
        )

    def raw(c, plane, kind, device):
        source = c_hbm.at[:, rows_of(c)] if kind < 2 else blocks.at[plane, :, rows_of(c)]
        return remote(source, blocks.at[plane, :, rows_of(c)], raw_send.at[kind], raw_recv.at[plane, c], device)

    def sum_copy(c, first=0, width=columns):
        here = remote_sum.at[:, rows_of(c), pl.ds(first, width)]
        return remote(here, here, sum_send, sum_recv.at[c], near)

    piece = 2 * b_hbm.shape[1] // n_alpha
    part = piece // PIECES

    def part_of(label, q):
        return pl.ds(pl.multiple_of(sources[label] * piece + q * part, part), part)

    def tile_copy(q):
        row = alpha * piece + q * part
        which = lax.div(row, b_hbm.shape[1])
        tile = (1 - which) * 2 + which * (1 + 2 * side)
        source = b_hbm.at[tile, pl.ds(pl.multiple_of(lax.rem(row, b_hbm.shape[1]), part), part)]
        return remote(source, outer_tiles.at[part_of(0, q)], tile_send, tile_recv.at[q], near)

    def group_of(label):
        return label.bit_count() - 1 if label < n_chips else rounds

    def tile_spread(q, label, target, device):
        here = outer_tiles.at[part_of(label, q)]
        recv = spread_recv.at[q // 2, group_of(target)] if target < n_chips else spread_last
        return remote(here, here, spread_send, recv, device)

    def held_spread(c, label, target, device):
        return remote(
            held[c].at[label], held[c].at[target], send_sem, recv_sem.at[c, group_of(target)], device
        )

    def spread(make, index, label):
        for step in range(label.bit_length(), rounds):
            make(index, label, label + 2**step, neighbours[step]).start()
        make(index, label, n_chips + label, sibling).start()

    labels_of = [range(1, n_chips - 1), range(n_chips - 1, n_chips), range(n_chips, n_alpha)]

    def tile_relay(pair, group):
        count = 2 * len(labels_of[group]) * part
        here = outer_tiles.at[pl.ds(0, count)]
        remote(here, here, spread_send, spread_recv.at[pair, group], sibling).wait_recv()
        for q in (2 * pair, 2 * pair + 1):
            for label in labels_of[group]:
                spread(tile_spread, q, label)

    def held_arrive(c, group):
        labels = labels_of[group]
        here = held[c].at[pl.ds(labels[0], len(labels))]
        remote(here, here, send_sem, recv_sem.at[c, group], sibling).wait_recv()

    def set_weights():
        for copy in local[:3]:
            copy.wait()
        picked = []
        for slot, source in enumerate(sources):
            live = counts_ref[source, alpha] == 1
            picked.append(jnp.clip(exc_ref[0, source, alpha] - source * n_blocks, 0, n_blocks - 1))
            target = exc_ref[1, source, alpha] - alpha * n_blocks
            matrix = coupling_ref[exc_ref[2, source, alpha]]
            for block in range(n_blocks):
                keep = jnp.where(live & (target == block), 1.0, 0.0).astype(jnp.float32)
                value = (matrix.astype(jnp.float32) * keep).astype(jnp.bfloat16)
                at = (pl.ds(block * order, order), pl.ds(slot * LANES, LANES))
                for half in range(order // LANES - 1):
                    weights[(half, *at)] = value[:, half * LANES : (half + 1) * LANES]
                last_weights[at] = value[:, order - LANES :]
        return picked

    def product(first, count, planes, tile, store, before=False, start=0, stop=columns):
        at_rows = pl.ds(offsets[first], sum(heights[first : first + count]))

        @pl.loop(start // TILE, stop // TILE)
        def _(n):
            at = pl.ds(pl.multiple_of(n * TILE, TILE), TILE)
            value = None
            for k, plane in enumerate(planes):
                left = blocks[plane, :, at_rows].reshape(n_blocks * at_rows.size, columns)
                term = jnp.dot(left, tile(k, plane, at), preferred_element_type=jnp.float32)
                value = term if value is None else value + term
            value = value.reshape(n_blocks, at_rows.size, TILE)
            if before:
                value = value + partial[:, at_rows, at]
            store(at_rows, at, value)

    def own_tile(k, plane, at):
        return tiles[distance(plane), :, at]

    def far_tile(k, plane, at):
        return outer_tiles[pl.ds(k * columns, columns), at]

    def store_held(c):
        def store(at_rows, at, value):
            held[c][0, :, :, at] = value.astype(jnp.bfloat16)
        return store

    def store_sum(at_rows, at, value):
        remote_sum[:, at_rows, at] = value.astype(jnp.bfloat16)

    def store_partial(at_rows, at, value):
        partial[:, at_rows, at] = value

    def relay(c, group):
        held_arrive(c, group)
        for label in labels_of[group]:
            spread(held_spread, c, label)

    def finish(c, picked):
        held_arrive(c, rounds)
        half, within = offsets[c] // LANES, offsets[c] % LANES
        final = half == order // LANES - 1
        panel = last_gathered if final else gathered.at[half]
        for slot in range(n_alpha):
            panel[pl.ds(slot * LANES + within, heights[c])] = held[c][slot, picked[slot]]
        if within + heights[c] == LANES and not final:
            @pl.loop(0, columns // TILE)
            def _(n):
                at = pl.ds(pl.multiple_of(n * TILE, TILE), TILE)
                value = jnp.dot(weights[half], gathered[half, :, at], preferred_element_type=jnp.float32)
                if half == 0:
                    out_ref[:, at] = value
                else:
                    out_ref[:, at] += value

    def advance(group, last, picked):
        while progress[group] <= min(last, chunks - 1):
            if group < rounds:
                relay(progress[group], group)
            else:
                finish(progress[group], picked)
            progress[group] += 1

    def follow(c, lag, picked):
        for group in range(rounds):
            advance(group, c - lag - LAG * group, picked)
        advance(rounds, c - lag - LAG * (rounds - 1) - 1, picked)

    def end(picked):
        advance(rounds, chunks - 1 - 2 * LAG, picked)
        for group in range(rounds - 1):
            advance(group, chunks - 1, picked)
        advance(rounds - 1, chunks - 2 - LAG, picked)
        advance(rounds, chunks - 2 - LAG, picked)
        advance(rounds - 1, chunks - 1, picked)
        advance(rounds, chunks - 1, picked)
        total = (n_alpha - 1) * n_blocks * order // n_beta
        here = tiles.at[:, pl.ds(0, total)]
        remote(here, here, send_sem, recv_sem.at[0, 0], sibling).wait_send()

    def sent(ref, sem):
        remote(ref, ref, sem, sum_recv.at[0], near).wait_send()

    progress = [0] * (rounds + 1)

    @pl.when(is_outer)
    def _():
        def own(c):
            raw(c, outer, 0, near).start()

        for q in range(PIECES):
            if q == PIECES // 2:
                own(0)
            tile_copy(q).start()
        for c in range(1, chunks):
            own(c)
        picked = set_weights()
        local[3].wait()
        local[4].wait()

        def prepare(c, count):
            for k in range(c, c + count):
                raw(k, inner, 0, near).wait_recv()
            product(c, count, (outer, inner), own_tile, store_partial)

        def finish_raw(c):
            raw(c, across, 0, near).wait_recv()
            raw(c, beyond, 0, near).wait_recv()
            product(c, 1, (across, beyond), own_tile, store_held(c), before=True)
            spread(held_spread, c, 0)

        prepare(0, 2)
        prepare(2, 2)
        finish_raw(0)
        finish_raw(1)
        follow(1, 1, picked)
        for c in range(RAW, chunks):
            if c == 4:
                prepare(c, 2)
            if c >= SECOND:
                prepare(c, 1)
            sum_copy(c).wait_recv()
            held[c][0] = (
                partial[:, rows_of(c)] + remote_sum[:, rows_of(c)].astype(jnp.float32)
            ).astype(jnp.bfloat16)
            spread(held_spread, c, 0)
            follow(c, 1 if c <= RAW + 1 else LAG, picked)
        end(picked)
        sent(outer_tiles.at[pl.ds(0, piece)], tile_send)
        sent(blocks.at[outer], raw_send.at[0])

    progress = [0] * (rounds + 1)

    @pl.when(jnp.logical_not(is_outer))
    def _():
        def own_near(c):
            raw(c, inner, 0, near).start()

        def own_facing(c):
            raw(c, inner, 1, facing).start()

        for c in range(FIRST):
            if c < 3:
                own_near(c)
            own_facing(c)
        picked = set_weights()
        local[3].wait()
        local[4].wait()

        def prepare(c):
            for k in range(c, c + 2):
                raw(k, across, 1, facing).wait_recv()
            product(c, 2, (inner, across), own_tile, store_partial)

        def pass_on(c):
            if c < chunks:
                raw(c, outer, 0, near).wait_recv()
                raw(c, outer, 2, facing).start()
                if SECOND <= c + 1 < chunks:
                    own_facing(c + 1)

        def tile_own(pair):
            for q in (2 * pair, 2 * pair + 1):
                tile_copy(q).wait_recv()
                spread(tile_spread, q, 0)

        tile_pass = tile_relay

        def finish_held(c):
            product(c, 1, (outer, beyond), own_tile, store_held(c), before=True)
            spread(held_spread, c, 0)

        def send_beyond(c):
            raw(c, beyond, 2, facing).wait_recv()
            raw(c, beyond, 3, near).start()

        def hold(c, lag):
            if c >= FIRST and c % 2 == 0:
                product(c, min(2, chunks - c), (inner, across), own_tile, store_partial)
            finish_held(c)
            follow(c, lag, picked)

        def send_across(c):
            raw(c, across, 1, facing).wait_recv()
            raw(c, across, 3, near).start()

        tile_own(0)
        tile_own(1)
        send_across(0)
        send_across(1)
        own_near(3)
        product(0, 2, (inner, across), own_tile, store_partial)
        pass_on(0)
        own_facing(4)
        own_facing(5)
        tile_pass(0, 0)
        tile_own(2)
        tile_pass(1, 0)
        prepare(2)
        tile_own(3)
        tile_pass(0, 1)
        send_beyond(0)
        own_near(4)
        own_near(5)
        tile_pass(2, 0)
        pass_on(1)
        tile_pass(1, 1)
        product(0, 1, (outer, beyond), own_tile, store_held(0), before=True)
        tile_pass(3, 0)
        pass_on(2)
        spread(held_spread, 0, 0)
        tile_pass(2, 1)
        pass_on(3)
        send_beyond(1)
        tile_pass(3, 1)
        hold(1, 1)
        pass_on(4)
        here = outer_tiles.at[pl.ds(0, n_chips * piece)]
        remote(here, here, spread_send, spread_last, sibling).wait_recv()
        for c in range(RAW, chunks):
            if c >= FIRST:
                raw(c, across, 1, facing).wait_recv()
            raw(c, beyond, 2, facing).wait_recv()
            for first in range(0, columns, columns // 2):
                product(c, 1, (across, beyond), far_tile, store_sum, start=first, stop=first + columns // 2)
                sum_copy(c, first, columns // 2).start()
            if SECOND <= c + 1 < chunks:
                own_near(c + 1)
            pass_on(c + 3)
            if c == RAW:
                hold(c, 1)
            elif c > RAW + 1:
                hold(c - 1, LAG)
        hold(chunks - 1, LAG)
        end(picked)
        sent(outer_tiles.at[pl.ds(0, (n_alpha - 1) * piece)], spread_send)
        sent(remote_sum.at[:, pl.ds(offsets[RAW], order - offsets[RAW])], sum_send)
        for kind in range(3):
            sent(blocks.at[inner], raw_send.at[kind])
        sent(blocks.at[inner, :, pl.ds(0, offsets[2 * RAW])], raw_send.at[3])


def line_call(mesh, coefficients, couplings, exc_list, counts, beta_tiles):
    n_alpha, n_beta = mesh.shape["alpha"], mesh.shape["beta"]
    order = couplings.shape[1]
    rows, columns = coefficients.shape
    n_blocks = rows // order
    heights = [order * share // sum(SHARES) for share in SHARES]
    chunks = len(heights)
    rounds = (n_alpha // 2).bit_length() - 1
    hbm = pl.BlockSpec(memory_space=pl.ANY)
    dma = pltpu.SemaphoreType.DMA
    total, last_weights, last_gathered = pl.pallas_call(
        functools.partial(line_kernel, n_alpha, n_beta, rounds, heights),
        out_shape=[
            pltpu.VMEM((rows, columns), jnp.float32),
            pltpu.VMEM((rows, n_alpha * LANES), jnp.bfloat16),
            pltpu.VMEM((n_alpha * LANES, columns), jnp.bfloat16),
        ],
        in_specs=[hbm] * 5,
        out_specs=[pl.BlockSpec(memory_space=pltpu.VMEM)] * 3,
        scratch_shapes=[
            pltpu.SMEM((3, n_alpha, n_alpha), jnp.int32),
            pltpu.SMEM((n_alpha, n_alpha), jnp.int32),
            pltpu.VMEM(couplings.shape, jnp.bfloat16),
            pltpu.VMEM((order // LANES - 1, rows, n_alpha * LANES), jnp.bfloat16),
            pltpu.VMEM(beta_tiles.shape, jnp.bfloat16),
            pltpu.VMEM((n_beta, n_blocks, order, columns), jnp.bfloat16),
            pltpu.VMEM((2 * columns, columns), jnp.bfloat16),
            pltpu.VMEM((n_blocks, order, columns), jnp.float32),
            pltpu.VMEM((n_blocks, order, columns), jnp.bfloat16),
            [pltpu.VMEM((n_alpha, n_blocks, height, columns), jnp.bfloat16) for height in heights],
            pltpu.VMEM((order // LANES - 1, n_alpha * LANES, columns), jnp.bfloat16),
            dma((5,)),
            dma((4,)),
            dma((n_beta, chunks)),
            dma(()),
            dma((chunks,)),
            dma(()),
            dma((PIECES,)),
            dma(()),
            dma((PIECES // 2, rounds)),
            dma(()),
            dma(()),
            dma((chunks, rounds + 1)),
        ],
        compiler_params=pltpu.CompilerParams(
            collective_id=0, has_side_effects=True, vmem_limit_bytes=60 * 2**20
        ),
    )(
        exc_list.transpose(2, 0, 1),
        counts,
        couplings,
        coefficients.reshape(n_blocks, order, columns),
        beta_tiles,
    )
    return total + jnp.dot(last_weights, last_gathered, preferred_element_type=jnp.float32)


def solution(mesh):
    n_alpha, n_beta = mesh.shape["alpha"], mesh.shape["beta"]
    n_chips = n_alpha // 2
    rounds = n_chips.bit_length() - 1

    def per_device(coefficients, couplings, exc_list, counts, beta_tiles):
        order = couplings.shape[1]
        rows, columns = coefficients.shape
        n_blocks = rows // order
        n_stops = beta_tiles.shape[0]
        if n_alpha == 8 and n_beta == n_stops == 4:
            return line_call(mesh, coefficients, couplings, exc_list, counts, beta_tiles)
        widths, _ = split(columns)
        chunks = len(widths)
        vmem, smem = pl.BlockSpec(memory_space=pltpu.VMEM), pl.BlockSpec(memory_space=pltpu.SMEM)
        hbm = pl.BlockSpec(memory_space=pl.ANY)
        return pl.pallas_call(
            functools.partial(kernel, n_alpha, n_beta, rounds, chunks),
            out_shape=pltpu.VMEM((rows, columns), jnp.float32),
            in_specs=[smem, smem, vmem, hbm, hbm],
            out_specs=vmem,
            scratch_shapes=[
                pltpu.VMEM((rows, n_alpha * order), jnp.bfloat16),
                pltpu.VMEM((n_alpha * order, max(widths)), jnp.bfloat16),
                pltpu.VMEM(beta_tiles.shape, jnp.bfloat16),
                [pltpu.VMEM((n_alpha, n_blocks, order, width), jnp.bfloat16) for width in widths],
                [pltpu.VMEM((n_stops, rows, width), jnp.bfloat16) for width in widths],
                pltpu.SemaphoreType.DMA((chunks, n_alpha)),
                pltpu.SemaphoreType.DMA((chunks, n_alpha)),
                pltpu.SemaphoreType.DMA((chunks,)),
                pltpu.SemaphoreType.DMA((chunks, n_stops - 1)),
                pltpu.SemaphoreType.DMA((chunks, n_stops - 1)),
                pltpu.SemaphoreType.DMA(()),
            ],
            compiler_params=pltpu.CompilerParams(
                collective_id=0, has_side_effects=True, vmem_limit_bytes=48 * 2**20
            ),
        )(
            exc_list.transpose(2, 0, 1),
            counts,
            couplings,
            coefficients.reshape(n_blocks, order, columns),
            beta_tiles,
        )

    placed = (P("alpha", "beta"), P(), P(), P(), P(None, None, "beta"))
    return jax.shard_map(
        per_device, mesh=mesh, in_specs=placed, out_specs=P("alpha", "beta"), check_vma=False
    )
```
